32 devices in a mesh: grp: 2 (over x), tm: 8 (over z, y), blk: 2 (over core).
Axes of the slice: x: 2, y: 2, z: 4, core: 2. Of those that a mesh axis runs over, the one named last changes fastest.
Arguments:
- hyper_params: float32 [6], P('grp'), parts along dimension 0, as said below
- space_precision: float32 [256, 256], P('blk'), may hold values from -1 to 16, as said below
- data_precision: float32 [32, 256, 256], P(('grp', 'tm'), 'blk'), parts along dimension 0, may hold values from -1 to 4, as said below
- covariates: float32 [32, 32, 256], P(('grp', 'tm'), None, 'blk'), parts along dimension 0
- fixed_precision: float32 [64], P('grp'), parts along dimension 0, may hold values from 0.5 to 2
Outputs:
- day_covariance: float32 [32, 256, 256], P(('grp', 'tm'), 'blk'), parts along dimension 0
- day_gradients: float32 [3, 32], P(None, ('grp', 'tm')), parts along dimension 1
- fixed_covariance: float32 [64, 32], P('grp'), parts along dimension 0
The draws below stay inside these ranges and needn't reach their ends.
There are 2 independent parts, one for each index of `grp`. The reference program is written for one: setup_inputs(seed, part) draws one part's arguments, and reference() takes and returns one part's arrays. A program takes and returns all parts, laid end to end along the dimension named above; an argument that names none is the same for every part. Nothing has to cross between parts.
Inputs may be any that keep to these rules, and one draw needn't show every extreme that they name: `hyper_params`: entries 0 and 2 lie in -0.3 to 0.3; entry 1 equals atanh(1 - e) with e between 1.5 / 16 and 6 / 16. `space_precision`: symmetric positive definite. `data_precision`: each day's block is symmetric positive definite.
All inputs are finite; a program needn't handle non-finite values.
Results may differ from the reference program's by a relative error of at most 0.0003.
Values sent between devices are 32-bit elements; how exact they have to be, the bound alone decides.
A program may use at most 128 MiB of HBM per device.

```python
import math
import jax
import jax.numpy as jnp
from jax import lax

NODES = 256
FIXED = 32
DAYS = 16


def symmetric_blocks(key, count_blocks, extent):
    keys = jax.random.split(key, 2)
    raw_values = jax.random.uniform(keys[0], (count_blocks, extent, extent), jnp.float32, -1.0, 1.0)
    mixed = (raw_values + jnp.swapaxes(raw_values, 1, 2)) * (0.5 * 1.35 / math.sqrt(extent))
    uniform_part = jax.random.uniform(keys[1], (count_blocks, extent), jnp.float32)
    diagonal = 1.6 + 2.0 * uniform_part
    identity = jnp.eye(extent, dtype=jnp.float32)
    return mixed * (1.0 - identity) + diagonal[:, :, None] * identity


def draw_hyper_params(key, part):
    uniform_part = jax.random.uniform(jax.random.fold_in(key, 14), (3,), jnp.float32)
    edge_value = (3.0 + 3.0 * uniform_part[1]) / DAYS
    middle = 0.5 * jnp.log((2.0 - edge_value) / edge_value)
    others = -0.3 + 0.6 * uniform_part
    return jnp.stack([others[0], middle, others[2]])


def draw_space_precision(key, part):
    return 4.0 * symmetric_blocks(jax.random.fold_in(key, 11), 1, NODES)[0]


def draw_data_precision(key, part):
    level_value = 64.0 / (DAYS * DAYS)
    blocks = symmetric_blocks(jax.random.fold_in(key, 12), DAYS, NODES) * level_value
    return blocks


def draw_covariates(key, part):
    base = jax.random.normal(jax.random.fold_in(key, 13), (DAYS, FIXED, NODES), jnp.float32)
    rising = 1.0 + 2.0 * jnp.arange(DAYS, dtype=jnp.float32) / max(DAYS - 1, 1)
    scale_value = 0.0625 * math.sqrt(DAYS / NODES)
    return base * scale_value * rising[:, None, None]


def setup_inputs(seed: int = 0, part: int = 0) -> dict:
    key_of = jax.random.split(jax.random.key(seed), 6)
    part_keys = jax.random.split(jax.random.fold_in(key_of[5], part), 6)
    hyper_params = draw_hyper_params(jax.random.fold_in(jax.random.fold_in(key_of[5], part), 71), part)
    space_precision = draw_space_precision(jax.random.fold_in(key_of[5], 71), part)
    data_precision = draw_data_precision(jax.random.fold_in(jax.random.fold_in(key_of[5], part), 71), part)
    covariates = draw_covariates(jax.random.fold_in(jax.random.fold_in(key_of[5], part), 71), part)
    fixed_precision = jnp.clip(jnp.exp(jax.random.uniform(part_keys[4], (FIXED,), jnp.float32, math.log(0.5), math.log(2.0))), 0.5, 2.0)
    return dict(hyper_params=hyper_params, space_precision=space_precision, data_precision=data_precision, covariates=covariates, fixed_precision=fixed_precision)


HIGHEST = lax.Precision.HIGHEST

def product(multiplier, multiplicand):
    return jnp.dot(multiplier.astype(jnp.float32), multiplicand.astype(jnp.float32), precision=HIGHEST, preferred_element_type=jnp.float32)

def frobenius(matrix_one, matrix_two):
    return jnp.sum(matrix_one * matrix_two)

def inverse_full(matrix):
    factor = jnp.linalg.cholesky(matrix)
    identity = jnp.eye(matrix.shape[0], dtype=matrix.dtype)
    return jax.scipy.linalg.cho_solve((factor, True), identity)

def reference(hyper_params, space_precision, data_precision, covariates, fixed_precision):
    prior_scale = jnp.exp(hyper_params[0])
    correlation = jnp.tanh(hyper_params[1])
    noise_scale = jnp.exp(hyper_params[2])
    complement = 1.0 - correlation * correlation
    day_index = jnp.arange(DAYS)
    border = (day_index == 0) | (day_index == DAYS - 1)
    weight = jnp.where(border, 1.0, 1.0 + correlation * correlation)
    weight_rate = jnp.where(border, 0.0, 2.0 * correlation * complement)
    couple = -prior_scale * correlation * space_precision
    arrow_blocks = noise_scale * jnp.einsum('dfi,dij->dfj', covariates, data_precision, precision=HIGHEST)
    data_gram = jnp.einsum('dfj,dgj->fg', arrow_blocks, covariates, precision=HIGHEST)

    def forward(carried, inputs):
        pending_block, pending_side, schur_terms = carried
        observed_day, arrow_day, weight_day = inputs
        square = prior_scale * weight_day * space_precision + noise_scale * observed_day + pending_block
        side_link = arrow_day + pending_side
        inverse = inverse_full(square)
        side_inverse = product(side_link, inverse)
        next_block = -product(product(couple, inverse), couple.T)
        next_side = -product(side_inverse, couple.T)
        schur_terms = schur_terms - product(side_inverse, side_link.T)
        return ((next_block, next_side, schur_terms), (inverse, side_link))
    start_state = (jnp.zeros((NODES, NODES), space_precision.dtype), jnp.zeros((FIXED, NODES), space_precision.dtype), jnp.zeros((FIXED, FIXED), space_precision.dtype))
    final_state, saved = lax.scan(forward, start_state, (data_precision, arrow_blocks, weight))
    inverses, side_links = saved
    schur_matrix = jnp.diag(fixed_precision) + data_gram + final_state[2]
    fixed_sigma = inverse_full(schur_matrix)

    def backward(carried, inputs):
        next_self, next_side = carried
        inverse, side_link, observed_day, arrow_day = inputs
        cross = -product(inverse, product(couple.T, next_self) + product(side_link.T, next_side))
        side_sigma = -product(product(next_side, couple) + product(fixed_sigma, side_link), inverse)
        self_sigma = inverse - product(product(cross, couple) + product(side_sigma.T, side_link), inverse)
        stats = jnp.stack([frobenius(self_sigma, space_precision), frobenius(self_sigma, observed_day), frobenius(side_sigma, arrow_day), frobenius(cross.T, space_precision)])
        return ((self_sigma, side_sigma), (self_sigma, stats))
    back_start = (jnp.zeros((NODES, NODES), space_precision.dtype), jnp.zeros((FIXED, NODES), space_precision.dtype))
    back_state, outputs = lax.scan(backward, back_start, (inverses, side_links, data_precision, arrow_blocks), reverse=True)
    day_sigma, stats = outputs
    trace_space = stats[:, 0]
    trace_data = stats[:, 1]
    trace_side = stats[:, 2]
    trace_cross = jnp.concatenate([jnp.zeros((1,), stats.dtype), stats[:-1, 3]], 0)
    gradients = jnp.stack([prior_scale * weight * trace_space - 2.0 * prior_scale * correlation * trace_cross, prior_scale * weight_rate * trace_space - 2.0 * prior_scale * complement * trace_cross, noise_scale * trace_data + 2.0 * trace_side]) / NODES
    return (day_sigma, gradients, fixed_sigma)
```

```python
import functools

import jax
import jax.numpy as jnp
from jax import lax
from jax.experimental import pallas as pl
from jax.experimental.pallas import tpu as pltpu
from jax.sharding import PartitionSpec as P

HIGHEST = lax.Precision.HIGHEST
F32 = jnp.float32
BF16 = jnp.bfloat16
VMEM = pl.BlockSpec(memory_space=pltpu.VMEM)
SMEM = pl.BlockSpec(memory_space=pltpu.SMEM)
ANY = pl.BlockSpec(memory_space=pl.ANY)
CLOSE = 1e-6
STEPS = 40
MESH = pl.DeviceIdType.MESH
MIB = 1024 * 1024


def split(a):
    high = a.astype(BF16)
    return high, (a - high.astype(F32)).astype(BF16)


def bdot(a, b):
    return jnp.dot(a.astype(BF16), b.astype(BF16), preferred_element_type=F32)


def contract(dims):
    def dot(a, b):
        def one(p, q):
            return lax.dot_general(p, q, (dims, ((), ())), preferred_element_type=F32)

        ah, al = split(a)
        bh, bl = split(b)
        return one(ah, bh) + (one(ah, bl) + one(al, bh))

    return dot


nn = contract(((1,), (0,)))
nt = contract(((1,), (1,)))
tn = contract(((0,), (0,)))


def full_dot(a, b):
    return jnp.dot(a, b, precision=HIGHEST, preferred_element_type=F32)


def diagonal(n):
    return lax.broadcasted_iota(jnp.int32, (n, n), 0) == lax.broadcasted_iota(jnp.int32, (n, n), 1)


def eye(n):
    return diagonal(n).astype(F32)


def squares(r):
    return jnp.sum(r * r)


def safe_start(a):
    unit = eye(a.shape[0])
    diag_row = jnp.sum(a * unit, axis=0, keepdims=True)
    diag_col = jnp.sum(a * unit, axis=1, keepdims=True)
    scaled = jnp.abs(a) * lax.rsqrt(diag_row) * lax.rsqrt(diag_col)
    bound = jnp.max(jnp.sum(scaled, axis=0, keepdims=True))
    return unit / (diag_row * bound)


def series(x_ref, r_ref):
    def more(state):
        count, size = state
        return (count < 12) & (size > 1e-4)

    def step(state):
        count, _ = state
        r = r_ref[...].astype(BF16)
        x_ref[...] += jnp.dot(r, x_ref[...].astype(BF16), preferred_element_type=F32)
        r_new = jnp.dot(r, r, preferred_element_type=F32)
        r_ref[...] = r_new
        return count + 1, squares(r_new)

    lax.while_loop(more, step, (0, squares(r_ref[...])))


def polish(a, x_ref):
    unit = eye(a.shape[0])

    def more(state):
        count, size, before = state
        return (count < STEPS) & (size > CLOSE) & ((size < before) | (size > 0.5))

    def step(state):
        count, size, _ = state
        r = unit - full_dot(a, x_ref[...])
        new = squares(r)
        restart = (count == 0) & ~(new < 0.8)

        @pl.when(restart)
        def _():
            x_ref[...] = safe_start(a)

        @pl.when(jnp.logical_not(restart))
        def _():
            x_ref[...] += nn(x_ref[...], r)

        return count + 1, jnp.where(restart, 1e30, new), jnp.where(restart, 2e30, size)

    lax.while_loop(more, step, (0, jnp.float32(1e30), jnp.float32(2e30)))


def first_kernel(a_ref, x_ref, r_ref):
    a = a_ref[...]
    start = safe_start(a)
    x_ref[...] = start
    r_ref[...] = eye(a.shape[0]) - jnp.sum(start, axis=1, keepdims=True) * a
    series(x_ref, r_ref)
    polish(a, x_ref)


def exchange_kernel(hyper, space, data, cov, c_ref, k_ref, h_ref, z_ref, a_ref, s_ref, *sems):
    ssem, rsem, lsem = sems
    core = lax.axis_index("blk")
    position = lax.axis_index("tm")
    days = 2 * lax.axis_size("tm")
    peer = {"blk": 1 - core}
    half = space.shape[0]
    barrier = pltpu.get_barrier_semaphore()
    pl.semaphore_signal(barrier, inc=1, device_id=peer, device_id_type=MESH)
    own = pl.ds(pl.multiple_of(core * half, half), half)
    own_blocks = [
        (space, k_ref.at[own, :]),
        (data.at[core], h_ref.at[own, :]),
        (cov.at[core], z_ref.at[:, own]),
    ]
    local = [
        pltpu.make_async_copy(src, dst, lsem.at[i]) for i, (src, dst) in enumerate(own_blocks)
    ]
    for copy in local:
        copy.start()
    sends = [
        (space, k_ref.at[own, :]),
        (data.at[1 - core], h_ref.at[own, :]),
        (cov.at[1 - core], z_ref.at[:, own]),
    ]
    remote = [
        pltpu.make_async_remote_copy(
            src_ref=src,
            dst_ref=dst,
            send_sem=ssem.at[i],
            recv_sem=rsem.at[i],
            device_id=peer,
            device_id_type=MESH,
        )
        for i, (src, dst) in enumerate(sends)
    ]
    pl.semaphore_wait(barrier, 1)
    for copy in remote:
        copy.start()
    wide = c_ref.shape[1]
    tau = jnp.exp(jnp.full((1, wide), hyper[0], F32))
    rho = jnp.tanh(jnp.full((1, wide), hyper[1], F32))
    noise = jnp.exp(jnp.full((1, wide), hyper[2], F32))
    day = 2 * position + core
    border = (day == 0) | (day == days - 1)
    scale = tau * jnp.where(border, 1.0, 1.0 + rho * rho)
    blank = jnp.zeros((4, wide), F32)
    c_ref[...] = jnp.concatenate([tau, rho, noise, scale, blank], axis=0)
    for copy in local:
        copy.wait()
    for copy in remote:
        copy.wait()
    h = h_ref[...]
    a_ref[...] = scale * k_ref[...] + noise * h
    s_ref[...] = noise * nn(z_ref[...], h)


def growth(bound, steps):
    factors = [2.0 / (2.0 - bound)]
    size = bound / (2.0 - bound)
    for _ in range(steps):
        top = size * size
        factors.append(2.0 / (2.0 - top))
        size = top / (2.0 - top)
    return factors


def warm_inverse(a, old, delta, bound, steps):
    n = a.shape[0]
    diag = diagonal(n)
    c = growth(bound, steps)

    def shifted(factor, m):
        m = factor * m
        return jnp.where(diag, m + (1.0 - factor), m)

    e = shifted(c[0], nn(old, delta)).astype(BF16)
    p = (c[0] * c[1]) * (e.astype(F32) + eye(n))
    for step in range(1, steps):
        e = shifted(c[step], bdot(e, e)).astype(BF16)
        p = p + bdot(e, p)
        if step < steps - 1:
            p = c[step + 1] * p
    x = nn(p, old)
    residual = eye(n) - nn(x, a)
    return x + bdot(residual, x)


def pack(ref, x):
    half = x.shape[0] // 2
    row = lax.broadcasted_iota(jnp.int32, (half, half), 0)
    col = lax.broadcasted_iota(jnp.int32, (half, half), 1)
    first = x[:half, :half]
    ref[pl.ds(0, half), pl.ds(0, half)] = x[half:, :half]
    ref[pl.ds(0, half), pl.ds(half, half)] = jnp.where(row > col, first, x[half:, half:])
    line = jnp.sum(jnp.where(row == col, first, 0.0), axis=0, keepdims=True)
    ref[pl.ds(half, 8), :] = jnp.broadcast_to(jnp.concatenate([line, line], axis=1), (8, 2 * half))


def unpack(ref):
    half = ref.shape[-1] // 2
    row = lax.broadcasted_iota(jnp.int32, (half, half), 0)
    col = lax.broadcasted_iota(jnp.int32, (half, half), 1)
    low = ref[pl.ds(0, half), pl.ds(0, half)]
    fold = ref[pl.ds(0, half), pl.ds(half, half)]
    line = ref[pl.ds(half, 1), pl.ds(0, half)]
    turned = fold.T
    first = jnp.where(row > col, fold, jnp.where(row == col, line, turned))
    last = jnp.where(row > col, turned, fold)
    return jnp.concatenate(
        [jnp.concatenate([first, low.T], axis=1), jnp.concatenate([low, last], axis=1)], axis=0
    )


def total(m):
    return jnp.sum(jnp.sum(m, axis=0, keepdims=True), axis=1, keepdims=True)


def slots(levels):
    names = ["w0", "w1", "w2", "w3", "v0", "v1", "part", "n", "yn", "m", "ym", "x", "y", "g"]
    for level in range(levels):
        names += [f"{kind}{level}{side}" for kind in "xsl" for side in "ab"]
    return {name: i for i, name in enumerate(names)}


def main_kernel(levels, c_ref, k_ref, h_ref, z_ref, s0_ref, x0_ref, a0_ref, prior_ref, *rest):
    out_ref, grad_ref, fixed_ref = rest[:3]
    wo, wi, vo, vi, to, ti, xo, xi, so, si, lo, li = rest[3:15]
    qo, qi, yo, yi, parts, xfin, xhalf, yfin, ypeer, gtile, ssem, rsem, psend, precv = rest[15:]
    n = 1 << levels
    extent = k_ref.shape[0]
    core = lax.axis_index("blk")
    m = lax.axis_index("tm")
    half = out_ref.shape[1]
    f = s0_ref.shape[0]
    number = slots(levels)

    barrier = pltpu.get_barrier_semaphore()

    @pl.loop(1, 2 * n)
    def _(o):
        t = (2 * m + core + o) % (2 * n)
        pl.semaphore_signal(
            barrier, inc=1, device_id={"tm": t // 2, "blk": t % 2}, device_id_type=MESH
        )

    def copy(name, src, dst, chip, side):
        return pltpu.make_async_remote_copy(
            src_ref=src,
            dst_ref=dst,
            send_sem=ssem.at[number[name]],
            recv_sem=rsem.at[number[name]],
            device_id={"tm": (chip + n) % n, "blk": side},
            device_id_type=MESH,
        )

    pending = {0: [], 1: []}

    def send(own, name, src, dst, chip, side, flag=None):
        transfer = copy(name, src, dst, chip, side)
        if flag is None:
            transfer.start()
        else:
            pl.when(flag)(transfer.start)
        pending[own].append((transfer, flag))

    def receive(own, name, dst, flag=None):
        transfer = copy(name, dst, dst, m, 1 - own)
        if flag is None:
            transfer.wait_recv()
            return
        pl.when(flag)(transfer.wait_recv)

        @pl.when(jnp.logical_not(flag))
        def _():
            dst[...] = jnp.zeros_like(dst)

    def drain(own):
        for transfer, flag in pending[own]:
            if flag is None:
                transfer.wait_send()
            else:
                pl.when(flag)(transfer.wait_send)

    def packet(own, to, slot):
        return pltpu.make_async_remote_copy(
            src_ref=parts.at[m],
            dst_ref=parts.at[slot],
            send_sem=psend.at[to],
            recv_sem=precv.at[slot],
            device_id={"tm": to // 2, "blk": to % 2},
            device_id_type=MESH,
        )

    def couple():
        return (c_ref[0:1, :] * c_ref[1:2, :]) * k_ref[...]

    def odd():
        k = couple()
        x0 = x0_ref[...]
        s0 = s0_ref[...]
        p = nn(k, x0)
        pack(wo, nt(p, k))
        pl.semaphore_wait(barrier, 2 * n - 1)
        send(1, "w1", wo, wi.at[1], m + 1, 0, m + 1 < n)
        send(1, "w0", wo, wi.at[0], m, 0)
        vo[...] = nt(s0, p)
        send(1, "v1", vo, vi.at[1], m + 1, 0, m + 1 < n)
        send(1, "v0", vo, vi.at[0], m, 0)
        send(1, "w2", wo, wi.at[2], m - 1, 0, (m >= 1) & (m < n - 1))
        send(1, "w3", wo, wi.at[3], m + 2, 0, m + 2 < n)
        part = nt(s0, z_ref[...]) - nt(nn(s0, x0), s0)
        to[...] = fold(part)
        send(1, "part", to, ti, m, 0)
        receive(1, "m", qi.at[0])
        f_own = nt(nn(k, unpack(qi.at[0])), k)
        receive(1, "n", qi.at[1], m < n - 1)
        b_own = nt(nn(k, unpack(qi.at[1])), k)
        delta = f_own + b_own
        x = warm_inverse(a0_ref[...] - delta, x0, delta, 0.91 if levels < 4 else 0.98, levels + 1)
        xfin[...] = x
        swap(1)
        receive(1, "ym", yi.at[0])
        receive(1, "yn", yi.at[1], m < n - 1)
        s_left = nt(yi[0], k)
        s = s0 + s_left + nt(yi[1], k)
        y = nn(s, x)
        finish(1, x, y, f_own, s_left)

    def even():
        receive(0, "w1", wi.at[1], m >= 1)
        receive(0, "w0", wi.at[0])
        x0 = x0_ref[...]
        s0 = s0_ref[...]
        a0 = a0_ref[...]
        f_own = unpack(wi.at[1])
        b_own = unpack(wi.at[0])
        delta = f_own + b_own
        l = -f_own
        u = jnp.where(m < n - 1, -1.0, 0.0) * b_own
        receive(0, "v1", vi.at[1], m >= 1)
        receive(0, "v0", vi.at[0])
        pl.semaphore_wait(barrier, 2 * n - 1)
        s_left = vi[1]
        s_right = vi[0]
        s_first = s0 + s_left + s_right
        x = x0
        for level in range(levels + 1):
            d = 1 << level
            last = level == levels
            a = a0 - (f_own + b_own)
            if last:
                break
            so[level] = s0 + s_left + s_right
            send(0, f"s{level}a", so.at[level], si.at[2 * level], m + d, 0, m + d < n)
            send(0, f"s{level}b", so.at[level], si.at[2 * level + 1], m - d, 0, m >= d)
            x = warm_inverse(a, x, delta, 0.75, 3)
            pack(xo.at[level], x)
            send(0, f"x{level}a", xo.at[level], xi.at[2 * level], m + d, 0, m + d < n)
            send(0, f"x{level}b", xo.at[level], xi.at[2 * level + 1], m - d, 0, m >= d)
            if 0 < level < levels - 1:
                lo[2 * level - 2] = l
                lo[2 * level - 1] = u
                lr, ur = li.at[2 * level - 2], li.at[2 * level - 1]
                send(0, f"l{level}a", lo.at[2 * level - 2], lr, m + d, 0, m + d < n)
                send(0, f"l{level}b", lo.at[2 * level - 1], ur, m - d, 0, m >= d)
            receive(0, f"s{level}a", si.at[2 * level], m >= d)
            receive(0, f"s{level}b", si.at[2 * level + 1], m + d < n)
            receive(0, f"x{level}a", xi.at[2 * level], m >= d)
            receive(0, f"x{level}b", xi.at[2 * level + 1], m + d < n)
            p = nn(l, unpack(xi.at[2 * level]))
            q = nn(u, unpack(xi.at[2 * level + 1]))
            d_left = nt(p, l)
            d_right = nt(q, u)
            f_own = f_own + d_left
            b_own = b_own + d_right
            delta = d_left + d_right
            s_left = s_left - nt(si[2 * level], p)
            s_right = s_right - nt(si[2 * level + 1], q)
            if level < levels - 1:
                if level == 0:
                    receive(0, "w3", wi.at[3], m >= 2)
                    receive(0, "w2", wi.at[2], m < n - 2)
                    l_far = -unpack(wi.at[3])
                    u_far = -unpack(wi.at[2])
                else:
                    receive(0, f"l{level}a", lr, m >= d)
                    receive(0, f"l{level}b", ur, m + d < n)
                    l_far, u_far = lr[...], ur[...]
                l = -nn(p, l_far)
                u = -nn(q, u_far)
        ahead = warm_inverse(a0 - b_own, x0, b_own, 0.5, 2)
        pack(qo.at[1], ahead)
        send(0, "n", qo.at[1], qi.at[1], m - 1, 1, m >= 1)
        before = warm_inverse(a0 - f_own, x0, f_own, 0.5, 2)
        pack(qo.at[0], before)
        send(0, "m", qo.at[0], qi.at[0], m, 1)
        x = warm_inverse(a, x, delta, 0.5, 3)
        xfin[...] = x
        s = s0 + s_left + s_right
        y = nn(s, x)
        receive(0, "part", ti)
        own = nt(s0, z_ref[...]) - nt(y, s_first)
        parts[m] = fold(own) + ti[...]

        @pl.loop(1, 2 * n)
        def _(o):
            packet(0, (2 * m + o) % (2 * n), m).start()

        swap(0)
        yo[1] = nn(s0 + s_right, ahead)
        send(0, "yn", yo.at[1], yi.at[1], m - 1, 1, m >= 1)
        yo[0] = nn(s0 + s_left, before)
        send(0, "ym", yo.at[0], yi.at[0], m, 1)
        finish(0, x, y, f_own, s_left)

        @pl.loop(1, 2 * n)
        def _(o):
            packet(0, (2 * m + o) % (2 * n), m).wait_send()

    def swap(own):
        src = xfin.at[pl.ds((1 - own) * half, half), :]
        send(own, "x", src, xhalf, m, 1 - own)

    def finish(own, x, y, f_own, s_left):
        day = 2 * m + own
        yfin[...] = y
        send(own, "y", yfin, ypeer, m, 1 - own)
        k, h = k_ref[...], h_ref[...]
        yk = nn(y, k)
        yh = nn(y, h)
        yf = nn(y, f_own) + s_left
        k_sum, h_sum, f_sum = total(x * k), total(x * h), total(x * f_own)

        @pl.loop(1 - own, n)
        def _(o):
            packet(own, 2 * m, (m + o) % n).wait_recv()

        sigma = gauss_jordan(eye(f) * prior_ref[...] + unfold(jnp.sum(parts[...], axis=0), f))
        fixed_ref[...] = sigma
        v = nn(sigma, y)
        k_sum = k_sum + total(v * yk)
        h_sum = h_sum + total(v * yh)
        f_sum = f_sum + total(v * yf)
        u_sum = -total(v * s0_ref[...])
        grads = gradients_of(c_ref, k_sum, h_sum, f_sum, u_sum, day, 2 * n, extent)
        line = lax.broadcasted_iota(jnp.int32, (8, 128), 0)
        tile = jnp.where(line == 0, grads[0], jnp.where(line == 1, grads[1], grads[2]))
        gtile[own] = tile
        send(own, "g", gtile.at[own], gtile.at[own], m, 1 - own)
        rows = slice(own * half, (own + 1) * half)
        out_ref[own] = x[rows, :] + tn(y[:, rows], v)
        receive(own, "y", ypeer)
        y_peer = ypeer[...]
        update = tn(y_peer[:, rows], nn(sigma, y_peer))
        receive(own, "x", xhalf)
        out_ref[1 - own] = xhalf[...] + update
        receive(own, "g", gtile.at[1 - own])
        two = lax.broadcasted_iota(jnp.int32, (3, 2), 1)
        grad_ref[...] = jnp.where(two == 0, gtile[0, pl.ds(0, 3), 0:2], gtile[1, pl.ds(0, 3), 0:2])
        drain(own)

    pl.when(core == 1)(odd)
    pl.when(core == 0)(even)


def fold(t):
    n = t.shape[0]
    return jnp.concatenate([t[i : i + 8] for i in range(0, n, 8)], axis=1)


def unfold(t, n):
    return jnp.concatenate([t[:, i : i + n] for i in range(0, n * n // 8, n)], axis=0)


def gauss_jordan(m):
    n = m.shape[0]
    rows = lax.broadcasted_iota(jnp.int32, (n, n), 0)
    cols = lax.broadcasted_iota(jnp.int32, (n, n), 1)
    for k in range(n):
        row = m[k : k + 1, :]
        col = m[:, k : k + 1]
        inv = 1.0 / m[k : k + 1, k : k + 1]
        row_s = row * inv
        m_next = m - col * row_s
        m_next = jnp.where(rows == k, row_s, m_next)
        m_next = jnp.where(cols == k, -col * inv, m_next)
        m = jnp.where((rows == k) & (cols == k), inv, m_next)
    return m


def gradients_of(c_ref, k_sum, h_sum, f_sum, u_sum, day, days, extent):
    tau, rho, noise = c_ref[0:1, 0:1], c_ref[1:2, 0:1], c_ref[2:3, 0:1]
    comp = 1.0 - rho * rho
    chain = f_sum / (tau * rho)
    border = (day == 0) | (day == days - 1)
    a_day = jnp.where(border, 1.0, 1.0 + rho * rho)
    b_day = jnp.where(border, 0.0, 2.0 * rho * comp)
    return [
        (tau * a_day * k_sum - 2.0 * tau * rho * chain) / extent,
        (tau * b_day * k_sum - 2.0 * tau * comp * chain) / extent,
        (noise * h_sum + 2.0 * u_sum) / extent,
    ]


def shaped(*shapes):
    return [jax.ShapeDtypeStruct(s, F32) for s in shapes]


def on_device(hyper_params, space_precision, data_precision, covariates, fixed_precision):
    n = lax.axis_size("tm")
    levels = n.bit_length() - 1
    half, extent = space_precision.shape
    fixed = covariates.shape[1]
    square = (extent, extent)
    side = (fixed, extent)
    packed = (half + 8, extent)
    far = max(2 * (levels - 2), 2)
    c, k, h, z, a, s0 = pl.pallas_call(
        exchange_kernel,
        out_shape=shaped((8, extent), square, square, side, square, side),
        in_specs=[SMEM] + [ANY] * 3,
        out_specs=[VMEM] * 6,
        scratch_shapes=[pltpu.SemaphoreType.DMA((3,))] * 3,
        compiler_params=pltpu.CompilerParams(
            collective_id=0, has_side_effects=True, vmem_limit_bytes=16 * MIB
        ),
    )(hyper_params, space_precision, data_precision, covariates)
    x = pl.pallas_call(
        first_kernel,
        out_shape=shaped(square)[0],
        in_specs=[VMEM],
        out_specs=VMEM,
        scratch_shapes=[pltpu.VMEM(square, F32)],
        compiler_params=pltpu.CompilerParams(vmem_limit_bytes=16 * MIB),
    )(a)
    count = len(slots(levels))
    buffers = [
        packed,
        (4,) + packed,
        side,
        (2,) + side,
        (8, 4 * fixed),
        (8, 4 * fixed),
        (levels,) + packed,
        (2 * levels,) + packed,
        (levels,) + side,
        (2 * levels,) + side,
        (far,) + square,
        (far,) + square,
        (2,) + packed,
        (2,) + packed,
        (2,) + side,
        (2,) + side,
        (n, 8, 4 * fixed),
        square,
        (half, extent),
        side,
        side,
        (2, 8, 128),
    ]
    return pl.pallas_call(
        functools.partial(main_kernel, levels),
        out_shape=shaped((2, half, extent), (3, 2), (fixed, fixed)),
        in_specs=[VMEM] * 8,
        out_specs=[VMEM] * 3,
        scratch_shapes=[pltpu.VMEM(shape, F32) for shape in buffers]
        + [
            pltpu.SemaphoreType.DMA((count,)),
            pltpu.SemaphoreType.DMA((count,)),
            pltpu.SemaphoreType.DMA((2 * n,)),
            pltpu.SemaphoreType.DMA((n,)),
        ],
        compiler_params=pltpu.CompilerParams(
            collective_id=1, has_side_effects=True, vmem_limit_bytes=40 * MIB
        ),
    )(c, k, h, z, s0, x, a, fixed_precision[None])


def solution(mesh):
    in_specs = (
        P("grp"),
        P("blk", None),
        P(("grp", "tm"), "blk", None),
        P(("grp", "tm"), None, "blk"),
        P("grp"),
    )
    out_specs = (P(("grp", "tm"), "blk", None), P(None, ("grp", "tm")), P("grp", None))
    return jax.shard_map(
        on_device, mesh=mesh, in_specs=in_specs, out_specs=out_specs, check_vma=False
    )
```

```python
import functools

import jax
import jax.numpy as jnp
from jax import lax
from jax.experimental import pallas as pl
from jax.experimental.pallas import tpu as pltpu
from jax.sharding import PartitionSpec as P

HIGHEST = lax.Precision.HIGHEST
F32 = jnp.float32
BF16 = jnp.bfloat16
VMEM = pl.BlockSpec(memory_space=pltpu.VMEM)
HBM = pl.BlockSpec(memory_space=pltpu.HBM)
CLOSE = 1e-6
STEPS = 40
MESH = pl.DeviceIdType.MESH
MIB = 1024 * 1024


def split(a):
    high = a.astype(BF16)
    return high, (a - high.astype(F32)).astype(BF16)


def bdot(a, b):
    return jnp.dot(a.astype(BF16), b.astype(BF16), preferred_element_type=F32)


def contract(dims):
    def dot(a, b):
        def one(p, q):
            return lax.dot_general(p, q, (dims, ((), ())), preferred_element_type=F32)

        ah, al = split(a)
        bh, bl = split(b)
        return one(ah, bh) + (one(ah, bl) + one(al, bh))

    return dot


nn = contract(((1,), (0,)))
nt = contract(((1,), (1,)))
tn = contract(((0,), (0,)))


def full_dot(a, b):
    return jnp.dot(a, b, precision=HIGHEST, preferred_element_type=F32)


def diagonal(n):
    return lax.broadcasted_iota(jnp.int32, (n, n), 0) == lax.broadcasted_iota(jnp.int32, (n, n), 1)


def eye(n):
    return diagonal(n).astype(F32)


def squares(r):
    return jnp.sum(r * r)


def safe_start(a):
    unit = eye(a.shape[0])
    diag_row = jnp.sum(a * unit, axis=0, keepdims=True)
    diag_col = jnp.sum(a * unit, axis=1, keepdims=True)
    scaled = jnp.abs(a) * lax.rsqrt(diag_row) * lax.rsqrt(diag_col)
    bound = jnp.max(jnp.sum(scaled, axis=0, keepdims=True))
    return unit / (diag_row * bound)


def series(x_ref, r_ref):
    def more(state):
        count, size = state
        return (count < 12) & (size > 1e-4)

    def step(state):
        count, _ = state
        r = r_ref[...].astype(BF16)
        x_ref[...] += jnp.dot(r, x_ref[...].astype(BF16), preferred_element_type=F32)
        r_new = jnp.dot(r, r, preferred_element_type=F32)
        r_ref[...] = r_new
        return count + 1, squares(r_new)

    lax.while_loop(more, step, (0, squares(r_ref[...])))


def polish(a, x_ref):
    unit = eye(a.shape[0])

    def more(state):
        count, size, before = state
        return (count < STEPS) & (size > CLOSE) & ((size < before) | (size > 0.5))

    def step(state):
        count, size, _ = state
        r = unit - full_dot(a, x_ref[...])
        new = squares(r)
        restart = (count == 0) & ~(new < 0.8)

        @pl.when(restart)
        def _():
            x_ref[...] = safe_start(a)

        @pl.when(jnp.logical_not(restart))
        def _():
            x_ref[...] += nn(x_ref[...], r)

        return count + 1, jnp.where(restart, 1e30, new), jnp.where(restart, 2e30, size)

    lax.while_loop(more, step, (0, jnp.float32(1e30), jnp.float32(2e30)))


def first_kernel(a_ref, x_ref, r_ref):
    a = a_ref[...]
    n = a.shape[0]
    unit = eye(n)
    diag_row = jnp.sum(a * unit, axis=0, keepdims=True)
    diag_col = jnp.sum(a * unit, axis=1, keepdims=True)
    inv_col = 1.0 / diag_col
    turned = a * inv_col
    weight = n / total(turned * a * (1.0 / diag_row))
    e = unit - weight * turned
    p = unit + e
    for _ in range(3):
        e = e.astype(BF16)
        e = bdot(e, e)
        p = p + bdot(e, p)
    x = p * (weight / diag_row)
    x = x + bdot(unit - nn(x, a), x)
    residual = unit - nn(x, a)
    x_ref[...] = x + bdot(residual, x)

    @pl.when(jnp.logical_not(squares(residual) < 1e-5))
    def _():
        start = safe_start(a)
        x_ref[...] = start
        r_ref[...] = unit - jnp.sum(start, axis=1, keepdims=True) * a
        series(x_ref, r_ref)
        polish(a, x_ref)


def exchange_kernel(hyper, space, data, cov, c_ref, k_ref, h_ref, z_ref, a_ref, s_ref, *sems):
    hyper_s, ssem, rsem, lsem = sems
    core = lax.axis_index("blk")
    position = lax.axis_index("tm")
    days = 2 * lax.axis_size("tm")
    peer = {"blk": 1 - core}
    half = space.shape[0]
    barrier = pltpu.get_barrier_semaphore()
    pl.semaphore_signal(barrier, inc=1, device_id=peer, device_id_type=MESH)
    own = pl.ds(pl.multiple_of(core * half, half), half)
    own_blocks = [
        (space, k_ref.at[own, :]),
        (data.at[core], h_ref.at[own, :]),
        (cov.at[core], z_ref.at[:, own]),
        (hyper, hyper_s),
    ]
    local = [
        pltpu.make_async_copy(src, dst, lsem.at[i]) for i, (src, dst) in enumerate(own_blocks)
    ]
    for copy in local:
        copy.start()
    sends = [
        (space, k_ref.at[own, :]),
        (data.at[1 - core], h_ref.at[own, :]),
        (cov.at[1 - core], z_ref.at[:, own]),
    ]
    remote = [
        pltpu.make_async_remote_copy(
            src_ref=src,
            dst_ref=dst,
            send_sem=ssem.at[i],
            recv_sem=rsem.at[i],
            device_id=peer,
            device_id_type=MESH,
        )
        for i, (src, dst) in enumerate(sends)
    ]
    pl.semaphore_wait(barrier, 1)
    for copy in remote:
        copy.start()
    wide = c_ref.shape[1]
    local[3].wait()
    tau = jnp.exp(jnp.full((1, wide), hyper_s[0], F32))
    rho = jnp.tanh(jnp.full((1, wide), hyper_s[1], F32))
    noise = jnp.exp(jnp.full((1, wide), hyper_s[2], F32))
    day = 2 * position + core
    border = (day == 0) | (day == days - 1)
    scale = tau * jnp.where(border, 1.0, 1.0 + rho * rho)
    blank = jnp.zeros((4, wide), F32)
    c_ref[...] = jnp.concatenate([tau, rho, noise, scale, blank], axis=0)
    for copy in local[:3]:
        copy.wait()
    for copy in remote:
        copy.wait()
    h = h_ref[...]
    a_ref[...] = scale * k_ref[...] + noise * h
    s_ref[...] = noise * nn(z_ref[...], h)


def growth(bound, steps):
    factors = [2.0 / (2.0 - bound)]
    size = bound / (2.0 - bound)
    for _ in range(steps):
        top = size * size
        factors.append(2.0 / (2.0 - top))
        size = top / (2.0 - top)
    return factors


def warm_inverse(a, old, delta, bound, steps):
    n = a.shape[0]
    diag = diagonal(n)
    c = growth(bound, steps)

    def shifted(factor, m):
        m = factor * m
        return jnp.where(diag, m + (1.0 - factor), m)

    e = shifted(c[0], nn(old, delta)).astype(BF16)
    p = (c[0] * c[1]) * (e.astype(F32) + eye(n))
    for step in range(1, steps):
        e = shifted(c[step], bdot(e, e)).astype(BF16)
        p = p + bdot(e, p)
        if step < steps - 1:
            p = c[step + 1] * p
    x = nn(p, old)
    residual = eye(n) - nn(x, a)
    return x + bdot(residual, x)


def pack(ref, x):
    half = x.shape[0] // 2
    row = lax.broadcasted_iota(jnp.int32, (half, half), 0)
    col = lax.broadcasted_iota(jnp.int32, (half, half), 1)
    first = x[:half, :half]
    ref[pl.ds(0, half), pl.ds(0, half)] = x[half:, :half]
    ref[pl.ds(0, half), pl.ds(half, half)] = jnp.where(row > col, first, x[half:, half:])
    line = jnp.sum(jnp.where(row == col, first, 0.0), axis=0, keepdims=True)
    ref[pl.ds(half, 8), :] = jnp.broadcast_to(jnp.concatenate([line, line], axis=1), (8, 2 * half))


def unpack(ref):
    half = ref.shape[-1] // 2
    row = lax.broadcasted_iota(jnp.int32, (half, half), 0)
    col = lax.broadcasted_iota(jnp.int32, (half, half), 1)
    low = ref[pl.ds(0, half), pl.ds(0, half)]
    fold = ref[pl.ds(0, half), pl.ds(half, half)]
    line = ref[pl.ds(half, 1), pl.ds(0, half)]
    turned = fold.T
    first = jnp.where(row > col, fold, jnp.where(row == col, line, turned))
    last = jnp.where(row > col, turned, fold)
    return jnp.concatenate(
        [jnp.concatenate([first, low.T], axis=1), jnp.concatenate([low, last], axis=1)], axis=0
    )


def total(m):
    return jnp.sum(jnp.sum(m, axis=0, keepdims=True), axis=1, keepdims=True)


def slots(levels):
    names = ["w0", "w1", "w2", "w3", "v0", "v1", "part", "n", "yn", "m", "ym", "x", "y", "g", "sigma"]
    for level in range(levels):
        names += [f"{kind}{level}{side}" for kind in "xsl" for side in "ab"]
    return {name: i for i, name in enumerate(names)}


def main_kernel(levels, c_ref, k_ref, h_ref, z_ref, s0_ref, x0_ref, a0_ref, prior_ref, *rest):
    out_ref, grad_ref, fixed_ref = rest[:3]
    wo, wi, vo, vi, to, ti, xo, xi, so, si, lo, li = rest[3:15]
    qo, qi, yo, yi, parts, xfin, xhalf, yfin, ypeer, tiles, sig, ssem, rsem, psend, precv = rest[15:]
    n = 1 << levels
    extent = k_ref.shape[0]
    core = lax.axis_index("blk")
    m = lax.axis_index("tm")
    half = out_ref.shape[1]
    f = s0_ref.shape[0]
    number = slots(levels)

    barrier = pltpu.get_barrier_semaphore()

    @pl.loop(1, 2 * n)
    def _(o):
        t = (2 * m + core + o) % (2 * n)
        pl.semaphore_signal(
            barrier, inc=1, device_id={"tm": t // 2, "blk": t % 2}, device_id_type=MESH
        )

    def copy(name, src, dst, chip, side):
        return pltpu.make_async_remote_copy(
            src_ref=src,
            dst_ref=dst,
            send_sem=ssem.at[number[name]],
            recv_sem=rsem.at[number[name]],
            device_id={"tm": (chip + n) % n, "blk": side},
            device_id_type=MESH,
        )

    pending = {0: [], 1: []}

    def send(own, name, src, dst, chip, side, flag=None):
        transfer = copy(name, src, dst, chip, side)
        if flag is None:
            transfer.start()
        else:
            pl.when(flag)(transfer.start)
        pending[own].append((transfer, flag))

    def receive(own, name, dst, flag=None):
        transfer = copy(name, dst, dst, m, 1 - own)
        if flag is None:
            transfer.wait_recv()
            return
        pl.when(flag)(transfer.wait_recv)

        @pl.when(jnp.logical_not(flag))
        def _():
            dst[...] = jnp.zeros_like(dst)

    def drain(own):
        for transfer, flag in pending[own]:
            if flag is None:
                transfer.wait_send()
            else:
                pl.when(flag)(transfer.wait_send)

    def packet(to, slot):
        return pltpu.make_async_remote_copy(
            src_ref=parts.at[m],
            dst_ref=parts.at[slot],
            send_sem=psend.at[to],
            recv_sem=precv.at[slot],
            device_id={"tm": to, "blk": 0},
            device_id_type=MESH,
        )

    def couple():
        return (c_ref[0:1, :] * c_ref[1:2, :]) * k_ref[...]

    def odd():
        k = couple()
        x0 = x0_ref[...]
        s0 = s0_ref[...]
        p = nn(k, x0)
        pack(wo, nt(p, k))
        pl.semaphore_wait(barrier, 2 * n - 1)
        send(1, "w1", wo, wi.at[1], m + 1, 0, m + 1 < n)
        send(1, "w0", wo, wi.at[0], m, 0)
        vo[...] = nt(s0, p)
        send(1, "v1", vo, vi.at[1], m + 1, 0, m + 1 < n)
        send(1, "v0", vo, vi.at[0], m, 0)
        send(1, "w2", wo, wi.at[2], m - 1, 0, (m >= 1) & (m < n - 1))
        send(1, "w3", wo, wi.at[3], m + 2, 0, m + 2 < n)
        part = nt(s0, z_ref[...]) - nt(nn(s0, x0), s0)
        to[...] = fold(part)
        send(1, "part", to, ti, m, 0)
        bound, steps = (0.83, 3) if levels < 4 else (0.96, 4)
        receive(1, "m", qi.at[0])
        f_own = nt(nn(k, unpack(qi.at[0])), k)
        a = a0_ref[...] - f_own
        x = warm_inverse(a, x0, f_own, bound, steps)
        receive(1, "n", qi.at[1], m < n - 1)
        b_own = nt(nn(k, unpack(qi.at[1])), k)
        x = warm_inverse(a - b_own, x, b_own, bound, steps)
        xfin[...] = x
        swap(1)
        receive(1, "ym", yi.at[0])
        receive(1, "yn", yi.at[1], m < n - 1)
        s_left = nt(yi[0], k)
        s = s0 + s_left + nt(yi[1], k)
        y = nn(s, x)
        yfin[...] = y
        send(1, "y", yfin, ypeer, m, 0)
        share(1, x, y, f_own, s_left)
        receive(1, "sigma", sig)
        finish(1, x, y, unfold(sig[...], f))

    def even():
        receive(0, "w1", wi.at[1], m >= 1)
        receive(0, "w0", wi.at[0])
        x0 = x0_ref[...]
        s0 = s0_ref[...]
        a0 = a0_ref[...]
        f_own = unpack(wi.at[1])
        b_own = unpack(wi.at[0])
        delta = f_own + b_own
        a = a0 - delta
        x = warm_inverse(a, x0, delta, 0.75, 3)
        pl.semaphore_wait(barrier, 2 * n - 1)
        l = -f_own
        u = jnp.where(m < n - 1, -1.0, 0.0) * b_own
        for level in range(levels + 1):
            d = 1 << level
            if level < levels:
                pack(xo.at[level], x)
                send(0, f"x{level}a", xo.at[level], xi.at[2 * level], m + d, 0, m + d < n)
                send(0, f"x{level}b", xo.at[level], xi.at[2 * level + 1], m - d, 0, m >= d)
            else:
                ahead = warm_inverse(a0 - b_own, x0, b_own, 0.5, 2)
                pack(qo.at[1], ahead)
                send(0, "n", qo.at[1], qi.at[1], m - 1, 1, m >= 1)
                x = warm_inverse(a, x, delta, 0.5, 3)
                xfin[...] = x
                swap(0)
            if level == 0:
                receive(0, "v1", vi.at[1], m >= 1)
                receive(0, "v0", vi.at[0])
                s_left = vi[1]
                s_right = vi[0]
                s_first = s0 + s_left + s_right
            else:
                back = d // 2
                receive(0, f"s{level - 1}a", si.at[2 * level - 2], m >= back)
                receive(0, f"s{level - 1}b", si.at[2 * level - 1], m + back < n)
                s_left = s_left - nt(si[2 * level - 2], p)
                s_right = s_right - nt(si[2 * level - 1], q)
            s = s0 + s_left + s_right
            if level == levels:
                break
            if 0 < level < levels:
                if level == 1:
                    receive(0, "w3", wi.at[3], m >= 2)
                    receive(0, "w2", wi.at[2], m < n - 2)
                    l_far = -unpack(wi.at[3])
                    u_far = -unpack(wi.at[2])
                else:
                    lr, ur = li.at[2 * level - 4], li.at[2 * level - 3]
                    receive(0, f"l{level - 1}a", lr, m >= back)
                    receive(0, f"l{level - 1}b", ur, m + back < n)
                    l_far, u_far = lr[...], ur[...]
                l = -nn(p, l_far)
                u = -nn(q, u_far)
            so[level] = s
            send(0, f"s{level}a", so.at[level], si.at[2 * level], m + d, 0, m + d < n)
            send(0, f"s{level}b", so.at[level], si.at[2 * level + 1], m - d, 0, m >= d)
            if 0 < level < levels - 1:
                ls, us = lo.at[2 * level - 2], lo.at[2 * level - 1]
                ls[...] = l
                us[...] = u
                send(0, f"l{level}a", ls, li.at[2 * level - 2], m + d, 0, m + d < n)
                send(0, f"l{level}b", us, li.at[2 * level - 1], m - d, 0, m >= d)
            receive(0, f"x{level}a", xi.at[2 * level], m >= d)
            receive(0, f"x{level}b", xi.at[2 * level + 1], m + d < n)
            p = nn(l, unpack(xi.at[2 * level]))
            q = nn(u, unpack(xi.at[2 * level + 1]))
            d_left = nt(p, l)
            d_right = nt(q, u)
            f_own = f_own + d_left
            b_own = b_own + d_right
            delta = d_left + d_right
            a = a0 - (f_own + b_own)
            if level < levels - 1:
                x = warm_inverse(a, x, delta, 0.75, 3)
        y = nn(s, x)
        receive(0, "part", ti)
        own = nt(s0, z_ref[...]) - nt(y, s_first)
        parts[m] = fold(own) + ti[...]

        @pl.loop(1, n)
        def _(o):
            packet((m + o) % n, m).start()

        before = warm_inverse(a0 - f_own, x0, f_own, 0.5, 2)
        pack(qo.at[0], before)
        send(0, "m", qo.at[0], qi.at[0], m, 1)
        yo[1] = nn(s0 + s_right, ahead)
        send(0, "yn", yo.at[1], yi.at[1], m - 1, 1, m >= 1)
        yo[0] = nn(s0 + s_left, before)
        send(0, "ym", yo.at[0], yi.at[0], m, 1)
        yfin[...] = y
        send(0, "y", yfin, ypeer, m, 1)
        share(0, x, y, f_own, s_left)

        @pl.loop(1, n)
        def _(o):
            packet(m, (m + o) % n).wait_recv()

        sigma = spd_inverse(eye(f) * prior_ref[...] + unfold(jnp.sum(parts[...], axis=0), f))
        sig[...] = fold(sigma)
        send(0, "sigma", sig, sig, m, 1)
        finish(0, x, y, sigma)

        @pl.loop(1, n)
        def _(o):
            packet((m + o) % n, m).wait_send()

    def swap(own):
        src = xfin.at[pl.ds((1 - own) * half, half), :]
        send(own, "x", src, xhalf, m, 1 - own)

    def share(own, x, y, f_own, s_left):
        day = 2 * m + own
        k, h = k_ref[...], h_ref[...]
        grams = [nt(nn(y, k), y), nt(nn(y, h), y), nt(nn(y, f_own) + s_left, y), -nt(s0_ref[...], y)]
        sums = [total(x * k), total(x * h), total(x * f_own), jnp.zeros((1, 1), F32)]
        for i, gram in enumerate(gradients_of(c_ref, *grams, day, 2 * n, extent)):
            tiles[own, i] = fold(gram)
        base = gradients_of(c_ref, *sums, day, 2 * n, extent)
        line = lax.broadcasted_iota(jnp.int32, (8, 4 * f), 0)
        tiles[own, 3] = jnp.where(line == 0, base[0], jnp.where(line == 1, base[1], base[2]))
        send(own, "g", tiles.at[own], tiles.at[own], m, 1 - own)

    def finish(own, x, y, sigma):
        fixed_ref[...] = sigma
        rows = slice(own * half, (own + 1) * half)
        out_ref[own] = x[rows, :] + tn(y[:, rows], nn(sigma, y))
        receive(own, "y", ypeer)
        y_peer = ypeer[...]
        update = tn(y_peer[:, rows], nn(sigma, y_peer))
        receive(own, "x", xhalf)
        out_ref[1 - own] = xhalf[...] + update
        receive(own, "g", tiles.at[1 - own])
        flat = fold(sigma)
        row = lax.broadcasted_iota(jnp.int32, (3, 2), 0)
        two = lax.broadcasted_iota(jnp.int32, (3, 2), 1)
        grads = jnp.zeros((3, 2), F32)
        for side in range(2):
            for i in range(3):
                value = tiles[side, 3, i : i + 1, 0:1] + total(flat * tiles[side, i])
                grads = jnp.where((row == i) & (two == side), value, grads)
        grad_ref[...] = grads
        drain(own)

    pl.when(core == 1)(odd)
    pl.when(core == 0)(even)


def fold(t):
    n = t.shape[0]
    return jnp.concatenate([t[i : i + 8] for i in range(0, n, 8)], axis=1)


def unfold(t, n):
    return jnp.concatenate([t[:, i : i + n] for i in range(0, n * n // 8, n)], axis=0)


def small_inverse(a, b, c, d):
    scale = 1.0 / (a * d - b * c)
    return d * scale, -b * scale, -c * scale, a * scale


def small_product(x, y):
    return (
        x[0] * y[0] + x[1] * y[2],
        x[0] * y[1] + x[1] * y[3],
        x[2] * y[0] + x[3] * y[2],
        x[2] * y[1] + x[3] * y[3],
    )


def spd_inverse(m):
    n = m.shape[0]
    rows = lax.broadcasted_iota(jnp.int32, (n, n), 0)
    cols = lax.broadcasted_iota(jnp.int32, (n, n), 1)
    line = cols[0:1]
    diag = jnp.where(rows == cols, m, 0.0)
    scale = lax.rsqrt(jnp.sum(diag, axis=0, keepdims=True)) * lax.rsqrt(
        jnp.sum(diag, axis=1, keepdims=True)
    )
    m = m * scale
    for k in range(0, n, 4):
        col = [jnp.broadcast_to(m[:, k + i : k + i + 1], (n, n)) for i in range(4)]
        pivot = [[col[j][k + i : k + i + 1, :] for j in range(4)] for i in range(4)]
        row = []
        for i in range(4):
            r = m[k + i : k + i + 1, :]
            for j in range(4):
                r = jnp.where(line == k + j, 1.0 if i == j else 0.0, r)
            row.append(r)
        a, b, c, d = [
            (pivot[i][j], pivot[i][j + 1], pivot[i + 1][j], pivot[i + 1][j + 1])
            for i in (0, 2)
            for j in (0, 2)
        ]
        a_inv = small_inverse(*a)
        ca = small_product(c, a_inv)
        ab = small_product(a_inv, b)
        schur = small_inverse(*[x - y for x, y in zip(d, small_product(ca, b))])
        low0 = row[2] - (ca[0] * row[0] + ca[1] * row[1])
        low1 = row[3] - (ca[2] * row[0] + ca[3] * row[1])
        t2 = schur[0] * low0 + schur[1] * low1
        t3 = schur[2] * low0 + schur[3] * low1
        t0 = a_inv[0] * row[0] + a_inv[1] * row[1] - (ab[0] * t2 + ab[1] * t3)
        t1 = a_inv[2] * row[0] + a_inv[3] * row[1] - (ab[2] * t2 + ab[3] * t3)
        in_rows = (rows >= k) & (rows < k + 4)
        m = jnp.where(in_rows | ((cols >= k) & (cols < k + 4)), 0.0, m)
        for i, t in enumerate((t0, t1, t2, t3)):
            m = m - jnp.where(in_rows, jnp.where(rows == k + i, -1.0, 0.0), col[i]) * t
    return m * scale


def gradients_of(c_ref, k_sum, h_sum, f_sum, u_sum, day, days, extent):
    tau, rho, noise = c_ref[0:1, 0:1], c_ref[1:2, 0:1], c_ref[2:3, 0:1]
    comp = 1.0 - rho * rho
    chain = f_sum / (tau * rho)
    border = (day == 0) | (day == days - 1)
    a_day = jnp.where(border, 1.0, 1.0 + rho * rho)
    b_day = jnp.where(border, 0.0, 2.0 * rho * comp)
    return [
        (tau * a_day * k_sum - 2.0 * tau * rho * chain) / extent,
        (tau * b_day * k_sum - 2.0 * tau * comp * chain) / extent,
        (noise * h_sum + 2.0 * u_sum) / extent,
    ]


def store_kernel(day_ref, grad_ref, fixed_ref, day_out, grad_out, fixed_out, sem):
    pairs = [(day_ref, day_out), (grad_ref, grad_out), (fixed_ref, fixed_out)]
    copies = [pltpu.make_async_copy(src, dst, sem.at[i]) for i, (src, dst) in enumerate(pairs)]
    for copy in copies:
        copy.start()
    for copy in copies:
        copy.wait()


def shaped(*shapes):
    return [jax.ShapeDtypeStruct(s, F32) for s in shapes]


def on_device(hyper_params, space_precision, data_precision, covariates, fixed_precision):
    n = lax.axis_size("tm")
    levels = n.bit_length() - 1
    half, extent = space_precision.shape
    fixed = covariates.shape[1]
    square = (extent, extent)
    side = (fixed, extent)
    packed = (half + 8, extent)
    far = max(2 * (levels - 2), 2)
    c, k, h, z, a, s0 = pl.pallas_call(
        exchange_kernel,
        out_shape=shaped((8, extent), square, square, side, square, side),
        in_specs=[HBM] * 4,
        out_specs=[VMEM] * 6,
        scratch_shapes=[pltpu.SMEM((3,), F32)]
        + [pltpu.SemaphoreType.DMA((3,))] * 2
        + [pltpu.SemaphoreType.DMA((4,))],
        compiler_params=pltpu.CompilerParams(
            collective_id=0, has_side_effects=True, vmem_limit_bytes=16 * MIB
        ),
    )(hyper_params, space_precision, data_precision, covariates)
    x = pl.pallas_call(
        first_kernel,
        out_shape=shaped(square)[0],
        in_specs=[VMEM],
        out_specs=VMEM,
        scratch_shapes=[pltpu.VMEM(square, F32)],
        compiler_params=pltpu.CompilerParams(vmem_limit_bytes=16 * MIB),
    )(a)
    count = len(slots(levels))
    buffers = [
        packed,
        (4,) + packed,
        side,
        (2,) + side,
        (8, 4 * fixed),
        (8, 4 * fixed),
        (levels,) + packed,
        (2 * levels,) + packed,
        (levels,) + side,
        (2 * levels,) + side,
        (far,) + square,
        (far,) + square,
        (2,) + packed,
        (2,) + packed,
        (2,) + side,
        (2,) + side,
        (n, 8, 4 * fixed),
        square,
        (half, extent),
        side,
        side,
        (2, 4, 8, 4 * fixed),
        (8, 4 * fixed),
    ]
    results = pl.pallas_call(
        functools.partial(main_kernel, levels),
        out_shape=shaped((2, half, extent), (3, 2), (fixed, fixed)),
        in_specs=[VMEM] * 8,
        out_specs=[VMEM] * 3,
        scratch_shapes=[pltpu.VMEM(shape, F32) for shape in buffers]
        + [
            pltpu.SemaphoreType.DMA((count,)),
            pltpu.SemaphoreType.DMA((count,)),
            pltpu.SemaphoreType.DMA((n,)),
            pltpu.SemaphoreType.DMA((n,)),
        ],
        compiler_params=pltpu.CompilerParams(
            collective_id=1, has_side_effects=True, vmem_limit_bytes=40 * MIB
        ),
    )(c, k, h, z, s0, x, a, fixed_precision[None])
    return pl.pallas_call(
        store_kernel,
        out_shape=shaped((2, half, extent), (3, 2), (fixed, fixed)),
        in_specs=[VMEM] * 3,
        out_specs=[HBM] * 3,
        scratch_shapes=[pltpu.SemaphoreType.DMA((3,))],
        compiler_params=pltpu.CompilerParams(vmem_limit_bytes=4 * MIB),
    )(*results)


def solution(mesh):
    in_specs = (
        P("grp"),
        P("blk", None),
        P(("grp", "tm"), "blk", None),
        P(("grp", "tm"), None, "blk"),
        P("grp"),
    )
    out_specs = (P(("grp", "tm"), "blk", None), P(None, ("grp", "tm")), P("grp", None))
    return jax.shard_map(
        on_device, mesh=mesh, in_specs=in_specs, out_specs=out_specs, check_vma=False
    )
```

```python
import functools

import jax
import jax.numpy as jnp
from jax import lax
from jax.experimental import pallas as pl
from jax.experimental.pallas import tpu as pltpu
from jax.sharding import PartitionSpec as P

HIGHEST = lax.Precision.HIGHEST
F32 = jnp.float32
BF16 = jnp.bfloat16
VMEM = pl.BlockSpec(memory_space=pltpu.VMEM)
SMEM = pl.BlockSpec(memory_space=pltpu.SMEM)
HBM = pl.BlockSpec(memory_space=pltpu.HBM)
CLOSE = 1e-6
STEPS = 40
MESH = pl.DeviceIdType.MESH
MIB = 1024 * 1024
COST = 2**32


def split(a):
    high = a.astype(BF16)
    return high, (a - high.astype(F32)).astype(BF16)


def bdot(a, b):
    return jnp.dot(a.astype(BF16), b.astype(BF16), preferred_element_type=F32)


def contract(dims):
    def dot(a, b):
        def one(p, q):
            return lax.dot_general(p, q, (dims, ((), ())), preferred_element_type=F32)

        ah, al = split(a)
        bh, bl = split(b)
        return one(ah, bh) + (one(ah, bl) + one(al, bh))

    return dot


nn = contract(((1,), (0,)))
nt = contract(((1,), (1,)))
tn = contract(((0,), (0,)))


def full_dot(a, b):
    return jnp.dot(a, b, precision=HIGHEST, preferred_element_type=F32)


def diagonal(n):
    return lax.broadcasted_iota(jnp.int32, (n, n), 0) == lax.broadcasted_iota(jnp.int32, (n, n), 1)


def eye(n):
    return diagonal(n).astype(F32)


def squares(r):
    return jnp.sum(r * r)


def safe_start(a):
    unit = eye(a.shape[0])
    diag_row = jnp.sum(a * unit, axis=0, keepdims=True)
    diag_col = jnp.sum(a * unit, axis=1, keepdims=True)
    scaled = jnp.abs(a) * lax.rsqrt(diag_row) * lax.rsqrt(diag_col)
    bound = jnp.max(jnp.sum(scaled, axis=0, keepdims=True))
    return unit / (diag_row * bound)


def series(x_ref, r_ref):
    def more(state):
        count, size = state
        return (count < 12) & (size > 1e-4)

    def step(state):
        count, _ = state
        r = r_ref[...].astype(BF16)
        x_ref[...] += jnp.dot(r, x_ref[...].astype(BF16), preferred_element_type=F32)
        r_new = jnp.dot(r, r, preferred_element_type=F32)
        r_ref[...] = r_new
        return count + 1, squares(r_new)

    lax.while_loop(more, step, (0, squares(r_ref[...])))


def polish(a, x_ref):
    unit = eye(a.shape[0])

    def more(state):
        count, size, before = state
        return (count < STEPS) & (size > CLOSE) & ((size < before) | (size > 0.5))

    def step(state):
        count, size, _ = state
        r = unit - full_dot(a, x_ref[...])
        new = squares(r)
        restart = (count == 0) & ~(new < 0.8)

        @pl.when(restart)
        def _():
            x_ref[...] = safe_start(a)

        @pl.when(jnp.logical_not(restart))
        def _():
            x_ref[...] += nn(x_ref[...], r)

        return count + 1, jnp.where(restart, 1e30, new), jnp.where(restart, 2e30, size)

    lax.while_loop(more, step, (0, jnp.float32(1e30), jnp.float32(2e30)))


def first_kernel(a_ref, x_ref, r_ref):
    a = a_ref[...]
    n = a.shape[0]
    unit = eye(n)
    diag_row = jnp.sum(a * unit, axis=0, keepdims=True)
    diag_col = jnp.sum(a * unit, axis=1, keepdims=True)
    inv_col = 1.0 / diag_col
    turned = a * inv_col
    weight = n / total(turned * a * (1.0 / diag_row))
    e = unit - weight * turned
    p = unit + e
    for _ in range(3):
        e = e.astype(BF16)
        e = bdot(e, e)
        p = p + bdot(e, p)
    x = p * (weight / diag_row)
    x = x + bdot(unit - nn(x, a), x)
    residual = unit - nn(x, a)
    x_ref[...] = x + bdot(residual, x)

    @pl.when(jnp.logical_not(squares(residual) < 1e-5))
    def _():
        start = safe_start(a)
        x_ref[...] = start
        r_ref[...] = unit - jnp.sum(start, axis=1, keepdims=True) * a
        series(x_ref, r_ref)
        polish(a, x_ref)


def scalar_kernel(hyper, c_ref):
    day = 2 * lax.axis_index("tm") + lax.axis_index("blk")
    days = 2 * lax.axis_size("tm")
    wide = c_ref.shape[1]
    tau = jnp.exp(jnp.full((1, wide), hyper[0], F32))
    rho = jnp.tanh(jnp.full((1, wide), hyper[1], F32))
    noise = jnp.exp(jnp.full((1, wide), hyper[2], F32))
    border = (day == 0) | (day == days - 1)
    scale = tau * jnp.where(border, 1.0, 1.0 + rho * rho)
    blank = jnp.zeros((4, wide), F32)
    c_ref[...] = jnp.concatenate([tau, rho, noise, scale, blank], axis=0)


def exchange_kernel(c_ref, space, data, cov, k_ref, h_ref, z_ref, a_ref, s_ref, *sems):
    ssem, rsem, lsem = sems
    core = lax.axis_index("blk")
    peer = {"blk": 1 - core}
    half = space.shape[0]
    barrier = pltpu.get_barrier_semaphore()
    pl.semaphore_signal(barrier, inc=1, device_id=peer, device_id_type=MESH)
    own = pl.ds(pl.multiple_of(core * half, half), half)
    own_blocks = [
        (space, k_ref.at[own, :]),
        (data.at[core], h_ref.at[own, :]),
        (cov.at[core], z_ref.at[:, own]),
    ]
    local = [
        pltpu.make_async_copy(src, dst, lsem.at[i]) for i, (src, dst) in enumerate(own_blocks)
    ]
    for copy in local:
        copy.start()
    sends = [
        (space, k_ref.at[own, :]),
        (data.at[1 - core], h_ref.at[own, :]),
        (cov.at[1 - core], z_ref.at[:, own]),
    ]
    remote = [
        pltpu.make_async_remote_copy(
            src_ref=src,
            dst_ref=dst,
            send_sem=ssem.at[i],
            recv_sem=rsem.at[i],
            device_id=peer,
            device_id_type=MESH,
        )
        for i, (src, dst) in enumerate(sends)
    ]
    pl.semaphore_wait(barrier, 1)
    for copy in remote:
        copy.start()
    for copy in local:
        copy.wait()
    for copy in remote:
        copy.wait()
    h = h_ref[...]
    noise = c_ref[2:3, :]
    a_ref[...] = c_ref[3:4, :] * k_ref[...] + noise * h
    s_ref[...] = noise * nn(z_ref[...], h)


def growth(bound, steps):
    factors = [2.0 / (2.0 - bound)]
    size = bound / (2.0 - bound)
    for _ in range(steps):
        top = size * size
        factors.append(2.0 / (2.0 - top))
        size = top / (2.0 - top)
    return factors


def warm_inverse(a, old, delta, bound, steps):
    n = a.shape[0]
    diag = diagonal(n)
    c = growth(bound, steps)

    def shifted(factor, m):
        m = factor * m
        return jnp.where(diag, m + (1.0 - factor), m)

    e = shifted(c[0], nn(old, delta)).astype(BF16)
    p = (c[0] * c[1]) * (e.astype(F32) + eye(n))
    for step in range(1, steps):
        e = shifted(c[step], bdot(e, e)).astype(BF16)
        p = p + bdot(e, p)
        if step < steps - 1:
            p = c[step + 1] * p
    high, low = split(old)
    x = bdot(p, high) + bdot(p, low)
    residual = eye(n) - nn(x, a)
    return x + bdot(residual, x)


def pack(ref, x):
    half = x.shape[0] // 2
    row = lax.broadcasted_iota(jnp.int32, (half, half), 0)
    col = lax.broadcasted_iota(jnp.int32, (half, half), 1)
    first = x[:half, :half]
    ref[pl.ds(0, half), pl.ds(0, half)] = x[half:, :half]
    ref[pl.ds(0, half), pl.ds(half, half)] = jnp.where(row > col, first, x[half:, half:])
    line = jnp.sum(jnp.where(row == col, first, 0.0), axis=0, keepdims=True)
    ref[pl.ds(half, 8), :] = jnp.broadcast_to(jnp.concatenate([line, line], axis=1), (8, 2 * half))


def unpack(ref):
    half = ref.shape[-1] // 2
    row = lax.broadcasted_iota(jnp.int32, (half, half), 0)
    col = lax.broadcasted_iota(jnp.int32, (half, half), 1)
    low = ref[pl.ds(0, half), pl.ds(0, half)]
    fold = ref[pl.ds(0, half), pl.ds(half, half)]
    line = ref[pl.ds(half, 1), pl.ds(0, half)]
    turned = fold.T
    first = jnp.where(row > col, fold, jnp.where(row == col, line, turned))
    last = jnp.where(row > col, turned, fold)
    return jnp.concatenate(
        [jnp.concatenate([first, low.T], axis=1), jnp.concatenate([low, last], axis=1)], axis=0
    )


def total(m):
    return jnp.sum(jnp.sum(m, axis=0, keepdims=True), axis=1, keepdims=True)


def slots(levels):
    names = ["w0", "w1", "w2", "w3", "v0", "v1", "part", "n", "yn", "m", "ym", "x", "y", "g", "sigma"]
    for level in range(levels):
        names += [f"{kind}{level}{side}" for kind in "xsl" for side in "ab"]
    return {name: i for i, name in enumerate(names)}


def main_kernel(levels, c_ref, k_ref, h_ref, z_ref, s0_ref, x0_ref, a0_ref, prior_ref, *rest):
    out_ref, grad_ref, fixed_ref = rest[:3]
    wo, wi, vo, vi, to, ti, xo, xi, so, si, lo, li = rest[3:15]
    qo, qi, yo, yi, parts, xfin, xhalf, yfin, ypeer, tiles, sig, ssem, rsem, psend, precv = rest[15:]
    n = 1 << levels
    extent = k_ref.shape[0]
    core = lax.axis_index("blk")
    m = lax.axis_index("tm")
    half = out_ref.shape[1]
    f = s0_ref.shape[0]
    number = slots(levels)

    barrier = pltpu.get_barrier_semaphore()

    @pl.loop(1, 2 * n)
    def _(o):
        t = (2 * m + core + o) % (2 * n)
        pl.semaphore_signal(
            barrier, inc=1, device_id={"tm": t // 2, "blk": t % 2}, device_id_type=MESH
        )

    def copy(name, src, dst, chip, side):
        return pltpu.make_async_remote_copy(
            src_ref=src,
            dst_ref=dst,
            send_sem=ssem.at[number[name]],
            recv_sem=rsem.at[number[name]],
            device_id={"tm": (chip + n) % n, "blk": side},
            device_id_type=MESH,
        )

    pending = {0: [], 1: []}

    def send(own, name, src, dst, chip, side, flag=None):
        transfer = copy(name, src, dst, chip, side)
        if flag is None:
            transfer.start()
        else:
            pl.when(flag)(transfer.start)
        pending[own].append((transfer, flag))

    def receive(own, name, dst, flag=None):
        transfer = copy(name, dst, dst, m, 1 - own)
        if flag is None:
            transfer.wait_recv()
            return
        pl.when(flag)(transfer.wait_recv)

        @pl.when(jnp.logical_not(flag))
        def _():
            dst[...] = jnp.zeros_like(dst)

    def drain(own):
        for transfer, flag in pending[own]:
            if flag is None:
                transfer.wait_send()
            else:
                pl.when(flag)(transfer.wait_send)

    def packet(to, slot):
        return pltpu.make_async_remote_copy(
            src_ref=parts.at[m],
            dst_ref=parts.at[slot],
            send_sem=psend.at[to],
            recv_sem=precv.at[slot],
            device_id={"tm": to, "blk": 0},
            device_id_type=MESH,
        )

    def couple():
        return (c_ref[0:1, :] * c_ref[1:2, :]) * k_ref[...]

    def odd():
        k = couple()
        x0 = x0_ref[...]
        s0 = s0_ref[...]
        p = nn(k, x0)
        pack(wo, nt(p, k))
        pl.semaphore_wait(barrier, 2 * n - 1)
        send(1, "w1", wo, wi.at[1], m + 1, 0, m + 1 < n)
        send(1, "w0", wo, wi.at[0], m, 0)
        vo[...] = nt(s0, p)
        send(1, "v1", vo, vi.at[1], m + 1, 0, m + 1 < n)
        send(1, "v0", vo, vi.at[0], m, 0)
        send(1, "w2", wo, wi.at[2], m - 1, 0, (m >= 1) & (m < n - 1))
        send(1, "w3", wo, wi.at[3], m + 2, 0, m + 2 < n)
        part = nt(s0, z_ref[...]) - nt(nn(s0, x0), s0)
        to[...] = fold(part)
        send(1, "part", to, ti, m, 0)
        bound, steps = (0.83, 3) if levels < 4 else (0.96, 4)
        receive(1, "m", qi.at[0])
        f_own = nt(nn(k, unpack(qi.at[0])), k)
        a = a0_ref[...] - f_own
        x = warm_inverse(a, x0, f_own, bound, steps)
        receive(1, "n", qi.at[1], m < n - 1)
        b_own = nt(nn(k, unpack(qi.at[1])), k)
        x = warm_inverse(a - b_own, x, b_own, bound, steps)
        xfin[...] = x
        swap(1)
        receive(1, "ym", yi.at[0])
        receive(1, "yn", yi.at[1], m < n - 1)
        s_left = nt(yi[0], k)
        s = s0 + (s_left + nt(yi[1], k))
        y = nn(s, x)
        yfin[...] = y
        send(1, "y", yfin, ypeer, m, 0)
        share(1, x, y, f_own, s_left)
        receive(1, "sigma", sig)
        finish(1, x, y, unfold(sig[...], f))

    def even():
        receive(0, "w1", wi.at[1], m >= 1)
        receive(0, "w0", wi.at[0])
        x0 = x0_ref[...]
        s0 = s0_ref[...]
        a0 = a0_ref[...]
        f_own = unpack(wi.at[1])
        b_own = unpack(wi.at[0])
        delta = f_own + b_own
        a = a0 - delta
        x = warm_inverse(a, x0, delta, 0.75, 3)
        pl.semaphore_wait(barrier, 2 * n - 1)
        l = -f_own
        u = jnp.where(m < n - 1, -1.0, 0.0) * b_own
        for level in range(levels + 1):
            d = 1 << level
            if level < levels:
                pack(xo.at[level], x)
                send(0, f"x{level}a", xo.at[level], xi.at[2 * level], m + d, 0, m + d < n)
                send(0, f"x{level}b", xo.at[level], xi.at[2 * level + 1], m - d, 0, m >= d)
            else:
                ahead = warm_inverse(a0 - b_own, x0, b_own, 0.5, 2)
                pack(qo.at[1], ahead)
                send(0, "n", qo.at[1], qi.at[1], m - 1, 1, m >= 1)
                before = warm_inverse(a0 - f_own, x0, f_own, 0.5, 2)
                pack(qo.at[0], before)
                send(0, "m", qo.at[0], qi.at[0], m, 1)
                x = warm_inverse(a, x, delta, 0.5, 3)
                xfin[...] = x
                swap(0)
            if level == 0:
                receive(0, "v1", vi.at[1], m >= 1)
                receive(0, "v0", vi.at[0])
                s_left = vi[1]
                s_right = vi[0]
                s_first = s0 + s_left + s_right
            else:
                back = d // 2
                receive(0, f"s{level - 1}a", si.at[2 * level - 2], m >= back)
                receive(0, f"s{level - 1}b", si.at[2 * level - 1], m + back < n)
                s_left = s_left - nt(si[2 * level - 2], p)
                s_right = s_right - nt(si[2 * level - 1], q)
            s = s0 + s_left + s_right
            if level == levels:
                break
            if 0 < level < levels:
                if level == 1:
                    receive(0, "w3", wi.at[3], m >= 2)
                    receive(0, "w2", wi.at[2], m < n - 2)
                    l_far = -unpack(wi.at[3])
                    u_far = -unpack(wi.at[2])
                else:
                    lr, ur = li.at[2 * level - 4], li.at[2 * level - 3]
                    receive(0, f"l{level - 1}a", lr, m >= back)
                    receive(0, f"l{level - 1}b", ur, m + back < n)
                    l_far, u_far = lr[...], ur[...]
                l = -nn(p, l_far)
                u = -nn(q, u_far)
            so[level] = s
            send(0, f"s{level}a", so.at[level], si.at[2 * level], m + d, 0, m + d < n)
            send(0, f"s{level}b", so.at[level], si.at[2 * level + 1], m - d, 0, m >= d)
            if 0 < level < levels - 1:
                ls, us = lo.at[2 * level - 2], lo.at[2 * level - 1]
                ls[...] = l
                us[...] = u
                send(0, f"l{level}a", ls, li.at[2 * level - 2], m + d, 0, m + d < n)
                send(0, f"l{level}b", us, li.at[2 * level - 1], m - d, 0, m >= d)
            receive(0, f"x{level}a", xi.at[2 * level], m >= d)
            receive(0, f"x{level}b", xi.at[2 * level + 1], m + d < n)
            p = nn(l, unpack(xi.at[2 * level]))
            q = nn(u, unpack(xi.at[2 * level + 1]))
            d_left = nt(p, l)
            d_right = nt(q, u)
            f_own = f_own + d_left
            b_own = b_own + d_right
            delta = d_left + d_right
            a = a0 - (f_own + b_own)
            if level < levels - 1:
                x = warm_inverse(a, x, delta, 0.75, 3)
        y = nn(s, x)
        receive(0, "part", ti)
        own = nt(s0, z_ref[...]) - nt(y, s_first)
        parts[m] = fold(own) + ti[...]

        @pl.loop(1, n)
        def _(o):
            packet((m + o) % n, m).start()

        yo[1] = nn(s0 + s_right, ahead)
        send(0, "yn", yo.at[1], yi.at[1], m - 1, 1, m >= 1)
        yo[0] = nn(s0 + s_left, before)
        send(0, "ym", yo.at[0], yi.at[0], m, 1)
        yfin[...] = y
        send(0, "y", yfin, ypeer, m, 1)
        share(0, x, y, f_own, s_left)

        @pl.loop(1, n)
        def _(o):
            packet(m, (m + o) % n).wait_recv()

        sigma = spd_inverse(eye(f) * prior_ref[...] + unfold(jnp.sum(parts[...], axis=0), f))
        sig[...] = fold(sigma)
        send(0, "sigma", sig, sig, m, 1)
        finish(0, x, y, sigma)

        @pl.loop(1, n)
        def _(o):
            packet((m + o) % n, m).wait_send()

    def swap(own):
        src = xfin.at[pl.ds((1 - own) * half, half), :]
        send(own, "x", src, xhalf, m, 1 - own)

    def share(own, x, y, f_own, s_left):
        day = 2 * m + own
        k, h = k_ref[...], h_ref[...]
        sides = [nn(y, k), nn(y, h), nn(y, f_own) + s_left, -s0_ref[...]]
        gram = nt(jnp.concatenate(sides, axis=0), y)
        grams = [gram[i * f : (i + 1) * f] for i in range(4)]
        sums = [total(x * k), total(x * h), total(x * f_own), jnp.zeros((1, 1), F32)]
        for i, gram in enumerate(gradients_of(c_ref, *grams, day, 2 * n, extent)):
            tiles[own, i] = fold(gram)
        base = gradients_of(c_ref, *sums, day, 2 * n, extent)
        line = lax.broadcasted_iota(jnp.int32, (8, 4 * f), 0)
        tiles[own, 3] = jnp.where(line == 0, base[0], jnp.where(line == 1, base[1], base[2]))
        send(own, "g", tiles.at[own], tiles.at[own], m, 1 - own)

    def finish(own, x, y, sigma):
        fixed_ref[...] = sigma
        rows = slice(own * half, (own + 1) * half)
        out_ref[own] = x[rows, :] + tn(y[:, rows], nn(sigma, y))
        receive(own, "y", ypeer)
        y_peer = ypeer[...]
        update = tn(y_peer[:, rows], nn(sigma, y_peer))
        receive(own, "x", xhalf)
        out_ref[1 - own] = xhalf[...] + update
        receive(own, "g", tiles.at[1 - own])
        flat = fold(sigma)
        two = lax.broadcasted_iota(jnp.int32, (2, 3), 0)
        col = lax.broadcasted_iota(jnp.int32, (2, 3), 1)
        grads = jnp.zeros((2, 3), F32)
        for side in range(2):
            for i in range(3):
                value = tiles[side, 3, i : i + 1, 0:1] + total(flat * tiles[side, i])
                grads = jnp.where((col == i) & (two == side), value, grads)
        grad_ref[...] = grads
        drain(own)

    pl.when(core == 1)(odd)
    pl.when(core == 0)(even)


def fold(t):
    n = t.shape[0]
    return jnp.concatenate([t[i : i + 8] for i in range(0, n, 8)], axis=1)


def unfold(t, n):
    return jnp.concatenate([t[:, i : i + n] for i in range(0, n * n // 8, n)], axis=0)


def small_inverse(a, b, c, d):
    scale = 1.0 / (a * d - b * c)
    return d * scale, -b * scale, -c * scale, a * scale


def small_product(x, y):
    return (
        x[0] * y[0] + x[1] * y[2],
        x[0] * y[1] + x[1] * y[3],
        x[2] * y[0] + x[3] * y[2],
        x[2] * y[1] + x[3] * y[3],
    )


def spd_inverse(m):
    n = m.shape[0]
    rows = lax.broadcasted_iota(jnp.int32, (n, n), 0)
    cols = lax.broadcasted_iota(jnp.int32, (n, n), 1)
    line = cols[0:1]
    diag = jnp.where(rows == cols, m, 0.0)
    scale = lax.rsqrt(jnp.sum(diag, axis=0, keepdims=True)) * lax.rsqrt(
        jnp.sum(diag, axis=1, keepdims=True)
    )
    m = m * scale
    for k in range(0, n, 4):
        col = [jnp.broadcast_to(m[:, k + i : k + i + 1], (n, n)) for i in range(4)]
        pivot = [[col[j][k + i : k + i + 1, :] for j in range(4)] for i in range(4)]
        row = []
        for i in range(4):
            r = m[k + i : k + i + 1, :]
            for j in range(4):
                r = jnp.where(line == k + j, 1.0 if i == j else 0.0, r)
            row.append(r)
        a, b, c, d = [
            (pivot[i][j], pivot[i][j + 1], pivot[i + 1][j], pivot[i + 1][j + 1])
            for i in (0, 2)
            for j in (0, 2)
        ]
        a_inv = small_inverse(*a)
        ca = small_product(c, a_inv)
        ab = small_product(a_inv, b)
        schur = small_inverse(*[x - y for x, y in zip(d, small_product(ca, b))])
        low0 = row[2] - (ca[0] * row[0] + ca[1] * row[1])
        low1 = row[3] - (ca[2] * row[0] + ca[3] * row[1])
        t2 = schur[0] * low0 + schur[1] * low1
        t3 = schur[2] * low0 + schur[3] * low1
        t0 = a_inv[0] * row[0] + a_inv[1] * row[1] - (ab[0] * t2 + ab[1] * t3)
        t1 = a_inv[2] * row[0] + a_inv[3] * row[1] - (ab[2] * t2 + ab[3] * t3)
        in_rows = (rows >= k) & (rows < k + 4)
        m = jnp.where(in_rows | ((cols >= k) & (cols < k + 4)), 0.0, m)
        for i, t in enumerate((t0, t1, t2, t3)):
            m = m - jnp.where(in_rows, jnp.where(rows == k + i, -1.0, 0.0), col[i]) * t
    return m * scale


def gradients_of(c_ref, k_sum, h_sum, f_sum, u_sum, day, days, extent):
    tau, rho, noise = c_ref[0:1, 0:1], c_ref[1:2, 0:1], c_ref[2:3, 0:1]
    comp = 1.0 - rho * rho
    chain = f_sum / (tau * rho)
    border = (day == 0) | (day == days - 1)
    a_day = jnp.where(border, 1.0, 1.0 + rho * rho)
    b_day = jnp.where(border, 0.0, 2.0 * rho * comp)
    return [
        (tau * a_day * k_sum - 2.0 * tau * rho * chain) / extent,
        (tau * b_day * k_sum - 2.0 * tau * comp * chain) / extent,
        (noise * h_sum + 2.0 * u_sum) / extent,
    ]


def store_kernel(day_ref, grad_ref, fixed_ref, day_out, grad_out, fixed_out, sem):
    pairs = [(day_ref, day_out), (grad_ref, grad_out), (fixed_ref, fixed_out)]
    copies = [pltpu.make_async_copy(src, dst, sem.at[i]) for i, (src, dst) in enumerate(pairs)]
    for copy in copies:
        copy.start()
    for copy in copies:
        copy.wait()


def shaped(*shapes):
    return [jax.ShapeDtypeStruct(s, F32) for s in shapes]


def on_device(hyper_params, space_precision, data_precision, covariates, fixed_precision):
    n = lax.axis_size("tm")
    levels = n.bit_length() - 1
    half, extent = space_precision.shape
    fixed = covariates.shape[1]
    square = (extent, extent)
    side = (fixed, extent)
    packed = (half + 8, extent)
    far = max(2 * (levels - 2), 2)
    c = pl.pallas_call(
        scalar_kernel,
        out_shape=shaped((8, extent))[0],
        in_specs=[SMEM],
        out_specs=VMEM,
        compiler_params=pltpu.CompilerParams(vmem_limit_bytes=16 * MIB),
        cost_estimate=pl.CostEstimate(flops=COST, bytes_accessed=8 * extent, transcendentals=0),
    )(hyper_params)
    k, h, z, a, s0 = pl.pallas_call(
        exchange_kernel,
        out_shape=shaped(square, square, side, square, side),
        in_specs=[VMEM] + [HBM] * 3,
        out_specs=[VMEM] * 5,
        scratch_shapes=[pltpu.SemaphoreType.DMA((3,))] * 3,
        compiler_params=pltpu.CompilerParams(
            collective_id=0, has_side_effects=True, vmem_limit_bytes=16 * MIB
        ),
    )(c, space_precision, data_precision, covariates)
    x = pl.pallas_call(
        first_kernel,
        out_shape=shaped(square)[0],
        in_specs=[VMEM],
        out_specs=VMEM,
        scratch_shapes=[pltpu.VMEM(square, F32)],
        compiler_params=pltpu.CompilerParams(vmem_limit_bytes=16 * MIB),
    )(a)
    count = len(slots(levels))
    buffers = [
        packed,
        (4,) + packed,
        side,
        (2,) + side,
        (8, 4 * fixed),
        (8, 4 * fixed),
        (levels,) + packed,
        (2 * levels,) + packed,
        (levels,) + side,
        (2 * levels,) + side,
        (far,) + square,
        (far,) + square,
        (2,) + packed,
        (2,) + packed,
        (2,) + side,
        (2,) + side,
        (n, 8, 4 * fixed),
        square,
        (half, extent),
        side,
        side,
        (2, 4, 8, 4 * fixed),
        (8, 4 * fixed),
    ]
    results = pl.pallas_call(
        functools.partial(main_kernel, levels),
        out_shape=shaped((2, half, extent), (2, 3), (fixed, fixed)),
        in_specs=[VMEM] * 8,
        out_specs=[VMEM] * 3,
        scratch_shapes=[pltpu.VMEM(shape, F32) for shape in buffers]
        + [
            pltpu.SemaphoreType.DMA((count,)),
            pltpu.SemaphoreType.DMA((count,)),
            pltpu.SemaphoreType.DMA((n,)),
            pltpu.SemaphoreType.DMA((n,)),
        ],
        compiler_params=pltpu.CompilerParams(
            collective_id=1, has_side_effects=True, vmem_limit_bytes=40 * MIB
        ),
    )(c, k, h, z, s0, x, a, fixed_precision[None])
    days, grads, sigma = pl.pallas_call(
        store_kernel,
        out_shape=shaped((2, half, extent), (2, 3), (fixed, fixed)),
        in_specs=[VMEM] * 3,
        out_specs=[HBM] * 3,
        scratch_shapes=[pltpu.SemaphoreType.DMA((3,))],
        compiler_params=pltpu.CompilerParams(vmem_limit_bytes=4 * MIB),
    )(*results)
    return days, grads.T, sigma


def solution(mesh):
    in_specs = (
        P("grp"),
        P("blk", None),
        P(("grp", "tm"), "blk", None),
        P(("grp", "tm"), None, "blk"),
        P("grp"),
    )
    out_specs = (P(("grp", "tm"), "blk", None), P(None, ("grp", "tm")), P("grp", None))
    return jax.shard_map(
        on_device, mesh=mesh, in_specs=in_specs, out_specs=out_specs, check_vma=False
    )
```

```python
import functools

import jax
import jax.numpy as jnp
from jax import lax
from jax.experimental import pallas as pl
from jax.experimental.pallas import tpu as pltpu
from jax.sharding import PartitionSpec as P

HIGHEST = lax.Precision.HIGHEST
F32 = jnp.float32
BF16 = jnp.bfloat16
VMEM = pl.BlockSpec(memory_space=pltpu.VMEM)
SMEM = pl.BlockSpec(memory_space=pltpu.SMEM)
HBM = pl.BlockSpec(memory_space=pltpu.HBM)
CLOSE = 1e-6
STEPS = 40
MESH = pl.DeviceIdType.MESH
MIB = 1024 * 1024
COST = 2**32


def split(a):
    high = a.astype(BF16)
    return high, (a - high.astype(F32)).astype(BF16)


def bdot(a, b):
    return jnp.dot(a.astype(BF16), b.astype(BF16), preferred_element_type=F32)


def contract(dims):
    def dot(a, b):
        def one(p, q):
            return lax.dot_general(p, q, (dims, ((), ())), preferred_element_type=F32)

        ah, al = a if isinstance(a, tuple) else split(a)
        bh, bl = b if isinstance(b, tuple) else split(b)
        return one(ah, bh) + (one(ah, bl) + one(al, bh))

    return dot


nn = contract(((1,), (0,)))
nt = contract(((1,), (1,)))
tn = contract(((0,), (0,)))


def full_dot(a, b):
    return jnp.dot(a, b, precision=HIGHEST, preferred_element_type=F32)


def diagonal(n):
    return lax.broadcasted_iota(jnp.int32, (n, n), 0) == lax.broadcasted_iota(jnp.int32, (n, n), 1)


def eye(n):
    return diagonal(n).astype(F32)


def squares(r):
    return jnp.sum(r * r)


def safe_start(a):
    unit = eye(a.shape[0])
    diag_row = jnp.sum(a * unit, axis=0, keepdims=True)
    diag_col = jnp.sum(a * unit, axis=1, keepdims=True)
    scaled = jnp.abs(a) * lax.rsqrt(diag_row) * lax.rsqrt(diag_col)
    bound = jnp.max(jnp.sum(scaled, axis=0, keepdims=True))
    return unit / (diag_row * bound)


def series(x_ref, r_ref):
    def more(state):
        count, size = state
        return (count < 12) & (size > 1e-4)

    def step(state):
        count, _ = state
        r = r_ref[...].astype(BF16)
        x_ref[...] += jnp.dot(r, x_ref[...].astype(BF16), preferred_element_type=F32)
        r_new = jnp.dot(r, r, preferred_element_type=F32)
        r_ref[...] = r_new
        return count + 1, squares(r_new)

    lax.while_loop(more, step, (0, squares(r_ref[...])))


def polish(a, x_ref):
    unit = eye(a.shape[0])

    def more(state):
        count, size, before = state
        return (count < STEPS) & (size > CLOSE) & ((size < before) | (size > 0.5))

    def step(state):
        count, size, _ = state
        r = unit - full_dot(a, x_ref[...])
        new = squares(r)
        restart = (count == 0) & ~(new < 0.8)

        @pl.when(restart)
        def _():
            x_ref[...] = safe_start(a)

        @pl.when(jnp.logical_not(restart))
        def _():
            x_ref[...] += nn(x_ref[...], r)

        return count + 1, jnp.where(restart, 1e30, new), jnp.where(restart, 2e30, size)

    lax.while_loop(more, step, (0, jnp.float32(1e30), jnp.float32(2e30)))


def first_kernel(a_ref, x_ref, r_ref):
    a = a_ref[...]
    n = a.shape[0]
    unit = eye(n)
    diag_row = jnp.sum(a * unit, axis=0, keepdims=True)
    diag_col = jnp.sum(a * unit, axis=1, keepdims=True)
    inv_col = 1.0 / diag_col
    turned = a * inv_col
    weight = n / total(turned * a * (1.0 / diag_row))
    e = unit - weight * turned
    p = unit + e
    for _ in range(3):
        e = e.astype(BF16)
        e = bdot(e, e)
        p = p + bdot(e, p)
    x = p * (weight / diag_row)
    x = x + bdot(unit - nn(x, a), x)
    residual = unit - nn(x, a)
    x_ref[...] = x + bdot(residual, x)

    @pl.when(jnp.logical_not(squares(residual) < 1e-5))
    def _():
        start = safe_start(a)
        x_ref[...] = start
        r_ref[...] = unit - jnp.sum(start, axis=1, keepdims=True) * a
        series(x_ref, r_ref)
        polish(a, x_ref)


def scalar_kernel(hyper, c_ref):
    day = 2 * lax.axis_index("tm") + lax.axis_index("blk")
    days = 2 * lax.axis_size("tm")
    wide = c_ref.shape[1]
    tau = jnp.exp(jnp.full((1, wide), hyper[0], F32))
    rho = jnp.tanh(jnp.full((1, wide), hyper[1], F32))
    noise = jnp.exp(jnp.full((1, wide), hyper[2], F32))
    border = (day == 0) | (day == days - 1)
    scale = tau * jnp.where(border, 1.0, 1.0 + rho * rho)
    blank = jnp.zeros((4, wide), F32)
    c_ref[...] = jnp.concatenate([tau, rho, noise, scale, blank], axis=0)


def exchange_kernel(c_ref, space, data, cov, k_ref, h_ref, z_ref, a_ref, *sems):
    ssem, rsem, lsem = sems
    core = lax.axis_index("blk")
    peer = {"blk": 1 - core}
    half = space.shape[0]
    barrier = pltpu.get_barrier_semaphore()
    pl.semaphore_signal(barrier, inc=1, device_id=peer, device_id_type=MESH)
    own = pl.ds(pl.multiple_of(core * half, half), half)
    own_blocks = [
        (space, k_ref.at[own, :]),
        (data.at[core], h_ref.at[own, :]),
        (cov.at[core], z_ref.at[:, own]),
    ]
    local = [
        pltpu.make_async_copy(src, dst, lsem.at[i]) for i, (src, dst) in enumerate(own_blocks)
    ]
    for copy in local:
        copy.start()
    sends = [
        (space, k_ref.at[own, :]),
        (data.at[1 - core], h_ref.at[own, :]),
        (cov.at[1 - core], z_ref.at[:, own]),
    ]
    remote = [
        pltpu.make_async_remote_copy(
            src_ref=src,
            dst_ref=dst,
            send_sem=ssem.at[i],
            recv_sem=rsem.at[i],
            device_id=peer,
            device_id_type=MESH,
        )
        for i, (src, dst) in enumerate(sends)
    ]
    pl.semaphore_wait(barrier, 1)
    for copy in remote:
        copy.start()
    for copy in local:
        copy.wait()
    for copy in remote:
        copy.wait()
    h = h_ref[...]
    noise = c_ref[2:3, :]
    a_ref[...] = c_ref[3:4, :] * k_ref[...] + noise * h


def growth(bound, steps):
    factors = [2.0 / (2.0 - bound)]
    size = bound / (2.0 - bound)
    for _ in range(steps):
        top = size * size
        factors.append(2.0 / (2.0 - top))
        size = top / (2.0 - top)
    return factors


def warm_inverse(a, old, delta, bound, steps):
    n = a.shape[0]
    diag = diagonal(n)
    c = growth(bound, steps)

    def shifted(factor, m):
        m = factor * m
        return jnp.where(diag, m + (1.0 - factor), m)

    high, low = old if isinstance(old, tuple) else split(old)
    e = shifted(c[0], nn((high, low), delta)).astype(BF16)
    p = (c[0] * c[1]) * (e.astype(F32) + eye(n))
    for step in range(1, steps):
        e = shifted(c[step], bdot(e, e)).astype(BF16)
        p = p + bdot(e, p)
        if step < steps - 1:
            p = c[step + 1] * p
    x = bdot(p, high) + bdot(p, low)
    residual = eye(n) - nn(x, a)
    return x + bdot(residual, x)


def pack(ref, x):
    half = x.shape[0] // 2
    row = lax.broadcasted_iota(jnp.int32, (half, half), 0)
    col = lax.broadcasted_iota(jnp.int32, (half, half), 1)
    first = x[:half, :half]
    ref[pl.ds(0, half), pl.ds(0, half)] = x[half:, :half]
    ref[pl.ds(0, half), pl.ds(half, half)] = jnp.where(row > col, first, x[half:, half:])
    line = jnp.sum(jnp.where(row == col, first, 0.0), axis=0, keepdims=True)
    ref[pl.ds(half, 8), :] = jnp.broadcast_to(jnp.concatenate([line, line], axis=1), (8, 2 * half))


def unpack(ref):
    half = ref.shape[-1] // 2
    row = lax.broadcasted_iota(jnp.int32, (half, half), 0)
    col = lax.broadcasted_iota(jnp.int32, (half, half), 1)
    low = ref[pl.ds(0, half), pl.ds(0, half)]
    fold = ref[pl.ds(0, half), pl.ds(half, half)]
    line = ref[pl.ds(half, 1), pl.ds(0, half)]
    turned = fold.T
    first = jnp.where(row > col, fold, jnp.where(row == col, line, turned))
    last = jnp.where(row > col, turned, fold)
    return jnp.concatenate(
        [jnp.concatenate([first, low.T], axis=1), jnp.concatenate([low, last], axis=1)], axis=0
    )


def total(m):
    return jnp.sum(jnp.sum(m, axis=0, keepdims=True), axis=1, keepdims=True)


def slots(levels):
    names = ["w0", "w1", "w2", "w3", "v0", "v1", "part", "n", "yn", "m", "ym", "x", "y", "g", "sigma", "ea", "ex"]
    for level in range(levels):
        names += [f"{kind}{level}{side}" for kind in "xsl" for side in "ab"]
    return {name: i for i, name in enumerate(names)}


def main_kernel(levels, c_ref, k_ref, h_ref, z_ref, x0_ref, a0_ref, prior_ref, *rest):
    out_ref, grad_ref, fixed_ref = rest[:3]
    wo, wi, vo, vi, to, ti, xo, xi, so, si, lo, li = rest[3:15]
    qo, qi, yo, yi, parts, xfin, xhalf, yfin, ypeer, tiles, sig, ea, ex, s0_ref, ssem, rsem, psend, precv = rest[15:]
    n = 1 << levels
    extent = k_ref.shape[0]
    core = lax.axis_index("blk")
    m = lax.axis_index("tm")
    half = out_ref.shape[1]
    f = z_ref.shape[0]
    number = slots(levels)

    barrier = pltpu.get_barrier_semaphore()

    @pl.loop(1, 2 * n)
    def _(o):
        t = (2 * m + core + o) % (2 * n)
        pl.semaphore_signal(
            barrier, inc=1, device_id={"tm": t // 2, "blk": t % 2}, device_id_type=MESH
        )

    def copy(name, src, dst, chip, side):
        return pltpu.make_async_remote_copy(
            src_ref=src,
            dst_ref=dst,
            send_sem=ssem.at[number[name]],
            recv_sem=rsem.at[number[name]],
            device_id={"tm": (chip + n) % n, "blk": side},
            device_id_type=MESH,
        )

    pending = {0: [], 1: []}

    def send(own, name, src, dst, chip, side, flag=None):
        transfer = copy(name, src, dst, chip, side)
        if flag is None:
            transfer.start()
        else:
            pl.when(flag)(transfer.start)
        pending[own].append((transfer, flag))

    def receive(own, name, dst, flag=None):
        transfer = copy(name, dst, dst, m, 1 - own)
        if flag is None:
            transfer.wait_recv()
            return
        pl.when(flag)(transfer.wait_recv)

        @pl.when(jnp.logical_not(flag))
        def _():
            dst[...] = jnp.zeros_like(dst)

    def drain(own):
        for transfer, flag in pending[own]:
            if flag is None:
                transfer.wait_send()
            else:
                pl.when(flag)(transfer.wait_send)

    def packet(to, slot):
        return pltpu.make_async_remote_copy(
            src_ref=parts.at[m],
            dst_ref=parts.at[slot],
            send_sem=psend.at[to],
            recv_sem=precv.at[slot],
            device_id={"tm": to, "blk": 0},
            device_id_type=MESH,
        )

    def arrow():
        s0 = c_ref[2:3, :] * nn(z_ref[...], h_ref[...])
        s0_ref[...] = s0
        return s0

    def couple():
        return (c_ref[0:1, :] * c_ref[1:2, :]) * k_ref[...]

    def odd():
        k = couple()
        k_parts = split(k)
        x0 = x0_ref[...]
        p = nn(k_parts, x0)
        pack(wo, nt(p, k_parts))
        pl.semaphore_wait(barrier, 2 * n - 1)
        send(1, "w1", wo, wi.at[1], m + 1, 0, m + 1 < n)
        send(1, "w0", wo, wi.at[0], m, 0)
        s0 = arrow()
        vo[...] = nt(s0, p)
        send(1, "v1", vo, vi.at[1], m + 1, 0, m + 1 < n)
        send(1, "v0", vo, vi.at[0], m, 0)
        send(1, "w2", wo, wi.at[2], m - 1, 0, (m >= 1) & (m < n - 1))
        send(1, "w3", wo, wi.at[3], m + 2, 0, m + 2 < n)
        part = nt(s0, z_ref[...]) - nt(nn(s0, x0), s0)
        to[...] = fold(part)
        send(1, "part", to, ti, m, 0)
        bound, steps = (0.83, 3) if levels < 4 else (0.96, 4)
        receive(1, "ea", ea)
        receive(1, "ex", ex)
        receive(1, "m", qi.at[0])
        f_even = unpack(qi.at[0])
        before = warm_inverse(ea[...] - f_even, ex[...], f_even, 0.5, 2)
        f_own = nt(nn(k, before), k)
        a = a0_ref[...] - f_own
        x = warm_inverse(a, x0, f_own, bound, steps)
        receive(1, "ym", yi.at[0])
        s_left = nt(nn(yi[0], before), k)
        x_parts = split(x)
        receive(1, "n", qi.at[1], m < n - 1)
        b_own = nt(nn(k_parts, unpack(qi.at[1])), k_parts)
        receive(1, "yn", yi.at[1], m < n - 1)
        s = s0 + (s_left + nt(yi[1], k))
        x = warm_inverse(a - b_own, x_parts, b_own, bound, steps)
        xfin[...] = x
        swap(1)
        y = nn(s, x)
        yfin[...] = y
        send(1, "y", yfin, ypeer, m, 0)
        share(1, x, y, f_own, s_left)
        receive(1, "sigma", sig)
        finish(1, x, y, unfold(sig[...], f))

    def even():
        pl.semaphore_wait(barrier, 2 * n - 1)
        s0 = arrow()
        send(0, "ea", a0_ref, ea, m, 1)
        send(0, "ex", x0_ref, ex, m, 1)
        receive(0, "w1", wi.at[1], m >= 1)
        receive(0, "w0", wi.at[0])
        x0 = x0_ref[...]
        a0 = a0_ref[...]
        f_own = unpack(wi.at[1])
        b_own = unpack(wi.at[0])
        delta = f_own + b_own
        a = a0 - delta
        x = warm_inverse(a, x0, delta, 0.75, 3)
        l = -f_own
        u = jnp.where(m < n - 1, -1.0, 0.0) * b_own
        for level in range(levels + 1):
            d = 1 << level
            if level < levels:
                pack(xo.at[level], x)
                send(0, f"x{level}a", xo.at[level], xi.at[2 * level], m + d, 0, m + d < n)
                send(0, f"x{level}b", xo.at[level], xi.at[2 * level + 1], m - d, 0, m >= d)
            else:
                pack(qo.at[0], f_own)
                send(0, "m", qo.at[0], qi.at[0], m, 1)
                ahead = warm_inverse(a0 - b_own, x0, b_own, 0.5, 2)
                pack(qo.at[1], ahead)
                send(0, "n", qo.at[1], qi.at[1], m - 1, 1, m >= 1)
            if level == 0:
                receive(0, "v1", vi.at[1], m >= 1)
                receive(0, "v0", vi.at[0])
                s_left = vi[1]
                s_right = vi[0]
                s_first = s0 + s_left + s_right
            else:
                back = d // 2
                receive(0, f"s{level - 1}a", si.at[2 * level - 2], m >= back)
                receive(0, f"s{level - 1}b", si.at[2 * level - 1], m + back < n)
                s_left = s_left - nt(si[2 * level - 2], p)
                s_right = s_right - nt(si[2 * level - 1], q)
            s = s0 + s_left + s_right
            if level == levels:
                break
            so[level] = s
            send(0, f"s{level}a", so.at[level], si.at[2 * level], m + d, 0, m + d < n)
            send(0, f"s{level}b", so.at[level], si.at[2 * level + 1], m - d, 0, m >= d)
            if 0 < level < levels:
                if level == 1:
                    receive(0, "w3", wi.at[3], m >= 2)
                    receive(0, "w2", wi.at[2], m < n - 2)
                    l_far = -unpack(wi.at[3])
                    u_far = -unpack(wi.at[2])
                else:
                    lr, ur = li.at[2 * level - 4], li.at[2 * level - 3]
                    receive(0, f"l{level - 1}a", lr, m >= back)
                    receive(0, f"l{level - 1}b", ur, m + back < n)
                    l_far, u_far = lr[...], ur[...]
                l = -nn(p, l_far)
                u = -nn(q, u_far)
            if 0 < level < levels - 1:
                ls, us = lo.at[2 * level - 2], lo.at[2 * level - 1]
                ls[...] = l
                us[...] = u
                send(0, f"l{level}a", ls, li.at[2 * level - 2], m + d, 0, m + d < n)
                send(0, f"l{level}b", us, li.at[2 * level - 1], m - d, 0, m >= d)
            l_parts, u_parts, x_parts = split(l), split(u), split(x)
            receive(0, f"x{level}a", xi.at[2 * level], m >= d)
            receive(0, f"x{level}b", xi.at[2 * level + 1], m + d < n)
            p = nn(l_parts, unpack(xi.at[2 * level]))
            q = nn(u_parts, unpack(xi.at[2 * level + 1]))
            d_left = nt(p, l_parts)
            d_right = nt(q, u_parts)
            f_own = f_own + d_left
            b_own = b_own + d_right
            delta = d_left + d_right
            a = a - delta
            if level < levels - 1:
                x = warm_inverse(a, x_parts, delta, 0.75, 3)
        yo[1] = nn(s0 + s_right, ahead)
        send(0, "yn", yo.at[1], yi.at[1], m - 1, 1, m >= 1)
        yo[0] = s0 + s_left
        send(0, "ym", yo.at[0], yi.at[0], m, 1)
        x = warm_inverse(a, x, delta, 0.5, 3)
        xfin[...] = x
        swap(0)
        y = nn(s, x)
        receive(0, "part", ti)
        own = nt(s0, z_ref[...]) - nt(y, s_first)
        parts[m] = fold(own) + ti[...]

        @pl.loop(1, n)
        def _(o):
            packet((m + o) % n, m).start()

        yfin[...] = y
        send(0, "y", yfin, ypeer, m, 1)
        share(0, x, y, f_own, s_left)

        @pl.loop(1, n)
        def _(o):
            packet(m, (m + o) % n).wait_recv()

        sigma = spd_inverse(eye(f) * prior_ref[...] + unfold(jnp.sum(parts[...], axis=0), f))
        sig[...] = fold(sigma)
        send(0, "sigma", sig, sig, m, 1)
        finish(0, x, y, sigma)

        @pl.loop(1, n)
        def _(o):
            packet((m + o) % n, m).wait_send()

    def swap(own):
        src = xfin.at[pl.ds((1 - own) * half, half), :]
        send(own, "x", src, xhalf, m, 1 - own)

    def share(own, x, y, f_own, s_left):
        day = 2 * m + own
        k, h = k_ref[...], h_ref[...]
        sides = [nn(y, k), nn(y, h), nn(y, f_own) + s_left, -s0_ref[...]]
        gram = nt(jnp.concatenate(sides, axis=0), y)
        grams = [gram[i * f : (i + 1) * f] for i in range(4)]
        sums = [total(x * k), total(x * h), total(x * f_own), jnp.zeros((1, 1), F32)]
        for i, gram in enumerate(gradients_of(c_ref, *grams, day, 2 * n, extent)):
            tiles[own, i] = fold(gram)
        base = gradients_of(c_ref, *sums, day, 2 * n, extent)
        line = lax.broadcasted_iota(jnp.int32, (8, 4 * f), 0)
        tiles[own, 3] = jnp.where(line == 0, base[0], jnp.where(line == 1, base[1], base[2]))
        send(own, "g", tiles.at[own], tiles.at[own], m, 1 - own)

    def finish(own, x, y, sigma):
        fixed_ref[...] = sigma
        rows = slice(own * half, (own + 1) * half)
        out_ref[own] = x[rows, :] + tn(y[:, rows], nn(sigma, y))
        receive(own, "y", ypeer)
        y_peer = ypeer[...]
        update = tn(y_peer[:, rows], nn(sigma, y_peer))
        receive(own, "x", xhalf)
        out_ref[1 - own] = xhalf[...] + update
        receive(own, "g", tiles.at[1 - own])
        flat = fold(sigma)
        two = lax.broadcasted_iota(jnp.int32, (2, 3), 0)
        col = lax.broadcasted_iota(jnp.int32, (2, 3), 1)
        grads = jnp.zeros((2, 3), F32)
        for side in range(2):
            for i in range(3):
                value = tiles[side, 3, i : i + 1, 0:1] + total(flat * tiles[side, i])
                grads = jnp.where((col == i) & (two == side), value, grads)
        grad_ref[...] = grads
        drain(own)

    pl.when(core == 1)(odd)
    pl.when(core == 0)(even)


def fold(t):
    n = t.shape[0]
    return jnp.concatenate([t[i : i + 8] for i in range(0, n, 8)], axis=1)


def unfold(t, n):
    return jnp.concatenate([t[:, i : i + n] for i in range(0, n * n // 8, n)], axis=0)


def small_inverse(a, b, c, d):
    scale = 1.0 / (a * d - b * c)
    return d * scale, -b * scale, -c * scale, a * scale


def small_product(x, y):
    return (
        x[0] * y[0] + x[1] * y[2],
        x[0] * y[1] + x[1] * y[3],
        x[2] * y[0] + x[3] * y[2],
        x[2] * y[1] + x[3] * y[3],
    )


def spd_inverse(m):
    n = m.shape[0]
    rows = lax.broadcasted_iota(jnp.int32, (n, n), 0)
    cols = lax.broadcasted_iota(jnp.int32, (n, n), 1)
    line = cols[0:1]
    diag = jnp.where(rows == cols, m, 0.0)
    scale = lax.rsqrt(jnp.sum(diag, axis=0, keepdims=True)) * lax.rsqrt(
        jnp.sum(diag, axis=1, keepdims=True)
    )
    m = m * scale
    for k in range(0, n, 4):
        col = [jnp.broadcast_to(m[:, k + i : k + i + 1], (n, n)) for i in range(4)]
        pivot = [[col[j][k + i : k + i + 1, :] for j in range(4)] for i in range(4)]
        row = []
        for i in range(4):
            r = m[k + i : k + i + 1, :]
            for j in range(4):
                r = jnp.where(line == k + j, 1.0 if i == j else 0.0, r)
            row.append(r)
        a, b, c, d = [
            (pivot[i][j], pivot[i][j + 1], pivot[i + 1][j], pivot[i + 1][j + 1])
            for i in (0, 2)
            for j in (0, 2)
        ]
        a_inv = small_inverse(*a)
        ca = small_product(c, a_inv)
        ab = small_product(a_inv, b)
        schur = small_inverse(*[x - y for x, y in zip(d, small_product(ca, b))])
        low0 = row[2] - (ca[0] * row[0] + ca[1] * row[1])
        low1 = row[3] - (ca[2] * row[0] + ca[3] * row[1])
        t2 = schur[0] * low0 + schur[1] * low1
        t3 = schur[2] * low0 + schur[3] * low1
        t0 = a_inv[0] * row[0] + a_inv[1] * row[1] - (ab[0] * t2 + ab[1] * t3)
        t1 = a_inv[2] * row[0] + a_inv[3] * row[1] - (ab[2] * t2 + ab[3] * t3)
        in_rows = (rows >= k) & (rows < k + 4)
        m = jnp.where(in_rows | ((cols >= k) & (cols < k + 4)), 0.0, m)
        for i, t in enumerate((t0, t1, t2, t3)):
            m = m - jnp.where(in_rows, jnp.where(rows == k + i, -1.0, 0.0), col[i]) * t
    return m * scale


def gradients_of(c_ref, k_sum, h_sum, f_sum, u_sum, day, days, extent):
    tau, rho, noise = c_ref[0:1, 0:1], c_ref[1:2, 0:1], c_ref[2:3, 0:1]
    comp = 1.0 - rho * rho
    chain = f_sum / (tau * rho)
    border = (day == 0) | (day == days - 1)
    a_day = jnp.where(border, 1.0, 1.0 + rho * rho)
    b_day = jnp.where(border, 0.0, 2.0 * rho * comp)
    return [
        (tau * a_day * k_sum - 2.0 * tau * rho * chain) / extent,
        (tau * b_day * k_sum - 2.0 * tau * comp * chain) / extent,
        (noise * h_sum + 2.0 * u_sum) / extent,
    ]


def store_kernel(day_ref, grad_ref, fixed_ref, day_out, grad_out, fixed_out, sem):
    pairs = [(day_ref, day_out), (grad_ref, grad_out), (fixed_ref, fixed_out)]
    copies = [pltpu.make_async_copy(src, dst, sem.at[i]) for i, (src, dst) in enumerate(pairs)]
    for copy in copies:
        copy.start()
    for copy in copies:
        copy.wait()


def shaped(*shapes):
    return [jax.ShapeDtypeStruct(s, F32) for s in shapes]


def on_device(hyper_params, space_precision, data_precision, covariates, fixed_precision):
    n = lax.axis_size("tm")
    levels = n.bit_length() - 1
    half, extent = space_precision.shape
    fixed = covariates.shape[1]
    square = (extent, extent)
    side = (fixed, extent)
    packed = (half + 8, extent)
    far = max(2 * (levels - 2), 2)
    c = pl.pallas_call(
        scalar_kernel,
        out_shape=shaped((8, extent))[0],
        in_specs=[SMEM],
        out_specs=VMEM,
        compiler_params=pltpu.CompilerParams(vmem_limit_bytes=16 * MIB),
        cost_estimate=pl.CostEstimate(flops=COST, bytes_accessed=8 * extent, transcendentals=0),
    )(hyper_params)
    k, h, z, a = pl.pallas_call(
        exchange_kernel,
        out_shape=shaped(square, square, side, square),
        in_specs=[VMEM] + [HBM] * 3,
        out_specs=[VMEM] * 4,
        scratch_shapes=[pltpu.SemaphoreType.DMA((3,))] * 3,
        compiler_params=pltpu.CompilerParams(
            collective_id=0, has_side_effects=True, vmem_limit_bytes=16 * MIB
        ),
    )(c, space_precision, data_precision, covariates)
    x = pl.pallas_call(
        first_kernel,
        out_shape=shaped(square)[0],
        in_specs=[VMEM],
        out_specs=VMEM,
        scratch_shapes=[pltpu.VMEM(square, F32)],
        compiler_params=pltpu.CompilerParams(vmem_limit_bytes=16 * MIB),
    )(a)
    count = len(slots(levels))
    buffers = [
        packed,
        (4,) + packed,
        side,
        (2,) + side,
        (8, 4 * fixed),
        (8, 4 * fixed),
        (levels,) + packed,
        (2 * levels,) + packed,
        (levels,) + side,
        (2 * levels,) + side,
        (far,) + square,
        (far,) + square,
        (2,) + packed,
        (2,) + packed,
        (2,) + side,
        (2,) + side,
        (n, 8, 4 * fixed),
        square,
        (half, extent),
        side,
        side,
        (2, 4, 8, 4 * fixed),
        (8, 4 * fixed),
        square,
        square,
        side,
    ]
    results = pl.pallas_call(
        functools.partial(main_kernel, levels),
        out_shape=shaped((2, half, extent), (2, 3), (fixed, fixed)),
        in_specs=[VMEM] * 7,
        out_specs=[VMEM] * 3,
        scratch_shapes=[pltpu.VMEM(shape, F32) for shape in buffers]
        + [
            pltpu.SemaphoreType.DMA((count,)),
            pltpu.SemaphoreType.DMA((count,)),
            pltpu.SemaphoreType.DMA((n,)),
            pltpu.SemaphoreType.DMA((n,)),
        ],
        compiler_params=pltpu.CompilerParams(
            collective_id=1, has_side_effects=True, vmem_limit_bytes=40 * MIB
        ),
    )(c, k, h, z, x, a, fixed_precision[None])
    days, grads, sigma = pl.pallas_call(
        store_kernel,
        out_shape=shaped((2, half, extent), (2, 3), (fixed, fixed)),
        in_specs=[VMEM] * 3,
        out_specs=[HBM] * 3,
        scratch_shapes=[pltpu.SemaphoreType.DMA((3,))],
        compiler_params=pltpu.CompilerParams(vmem_limit_bytes=4 * MIB),
    )(*results)
    return days, grads.T, sigma


def solution(mesh):
    in_specs = (
        P("grp"),
        P("blk", None),
        P(("grp", "tm"), "blk", None),
        P(("grp", "tm"), None, "blk"),
        P("grp"),
    )
    out_specs = (P(("grp", "tm"), "blk", None), P(None, ("grp", "tm")), P("grp", None))
    return jax.shard_map(
        on_device, mesh=mesh, in_specs=in_specs, out_specs=out_specs, check_vma=False
    )
```

```python
import functools

import jax
import jax.numpy as jnp
from jax import lax
from jax.experimental import pallas as pl
from jax.experimental.pallas import tpu as pltpu
from jax.sharding import PartitionSpec as P

HIGHEST = lax.Precision.HIGHEST
F32 = jnp.float32
BF16 = jnp.bfloat16
VMEM = pl.BlockSpec(memory_space=pltpu.VMEM)
HBM = pl.BlockSpec(memory_space=pltpu.HBM)
CLOSE = 1e-6
STEPS = 40
MESH = pl.DeviceIdType.MESH
MIB = 1024 * 1024
COST = 2**32


def split(a):
    high = a.astype(BF16)
    return high, (a - high.astype(F32)).astype(BF16)


def bdot(a, b):
    return jnp.dot(a.astype(BF16), b.astype(BF16), preferred_element_type=F32)


def contract(dims):
    def dot(a, b):
        def one(p, q):
            return lax.dot_general(p, q, (dims, ((), ())), preferred_element_type=F32)

        ah, al = a if isinstance(a, tuple) else split(a)
        bh, bl = b if isinstance(b, tuple) else split(b)
        return one(ah, bh) + (one(ah, bl) + one(al, bh))

    return dot


nn = contract(((1,), (0,)))
nt = contract(((1,), (1,)))
tn = contract(((0,), (0,)))


def full_dot(a, b):
    return jnp.dot(a, b, precision=HIGHEST, preferred_element_type=F32)


def diagonal(n):
    return lax.broadcasted_iota(jnp.int32, (n, n), 0) == lax.broadcasted_iota(jnp.int32, (n, n), 1)


def eye(n):
    return diagonal(n).astype(F32)


def squares(r):
    return jnp.sum(r * r)


def safe_start(a):
    unit = eye(a.shape[0])
    diag_row = jnp.sum(a * unit, axis=0, keepdims=True)
    diag_col = jnp.sum(a * unit, axis=1, keepdims=True)
    scaled = jnp.abs(a) * lax.rsqrt(diag_row) * lax.rsqrt(diag_col)
    bound = jnp.max(jnp.sum(scaled, axis=0, keepdims=True))
    return unit / (diag_row * bound)


def series(x_ref, r_ref):
    def more(state):
        count, size = state
        return (count < 12) & (size > 1e-4)

    def step(state):
        count, _ = state
        r = r_ref[...].astype(BF16)
        x_ref[...] += jnp.dot(r, x_ref[...].astype(BF16), preferred_element_type=F32)
        r_new = jnp.dot(r, r, preferred_element_type=F32)
        r_ref[...] = r_new
        return count + 1, squares(r_new)

    lax.while_loop(more, step, (0, squares(r_ref[...])))


def polish(a, x_ref):
    unit = eye(a.shape[0])

    def more(state):
        count, size, before = state
        return (count < STEPS) & (size > CLOSE) & ((size < before) | (size > 0.5))

    def step(state):
        count, size, _ = state
        r = unit - full_dot(a, x_ref[...])
        new = squares(r)
        restart = (count == 0) & ~(new < 0.8)

        @pl.when(restart)
        def _():
            x_ref[...] = safe_start(a)

        @pl.when(jnp.logical_not(restart))
        def _():
            x_ref[...] += nn(x_ref[...], r)

        return count + 1, jnp.where(restart, 1e30, new), jnp.where(restart, 2e30, size)

    lax.while_loop(more, step, (0, jnp.float32(1e30), jnp.float32(2e30)))


def first_kernel(a_ref, x_ref, r_ref):
    a = a_ref[...]
    n = a.shape[0]
    unit = eye(n)
    diag_row = jnp.sum(a * unit, axis=0, keepdims=True)
    diag_col = jnp.sum(a * unit, axis=1, keepdims=True)
    inv_col = 1.0 / diag_col
    turned = a * inv_col
    weight = n / total(turned * a * (1.0 / diag_row))
    e = unit - weight * turned
    p = unit + e
    for _ in range(3):
        e = e.astype(BF16)
        e = bdot(e, e)
        p = p + bdot(e, p)
    x = p * (weight / diag_row)
    x = x + bdot(unit - nn(x, a), x)
    residual = unit - nn(x, a)
    x_ref[...] = x + bdot(residual, x)

    @pl.when(jnp.logical_not(squares(residual) < 1e-5))
    def _():
        start = safe_start(a)
        x_ref[...] = start
        r_ref[...] = unit - jnp.sum(start, axis=1, keepdims=True) * a
        series(x_ref, r_ref)
        polish(a, x_ref)


def ready_kernel(ready_ref):
    ready_ref[...] = jnp.zeros_like(ready_ref)


def exchange_kernel(ready_ref, hyper, space, data, cov, c_ref, k_ref, h_ref, z_ref, a_ref, *sems):
    ssem, rsem, lsem = sems
    core = lax.axis_index("blk")
    peer = {"blk": 1 - core}
    half = space.shape[0]
    barrier = pltpu.get_barrier_semaphore()
    pl.semaphore_signal(barrier, inc=1, device_id=peer, device_id_type=MESH)
    own = pl.ds(pl.multiple_of(core * half, half), half)
    own_blocks = [
        (space, k_ref.at[own, :]),
        (data.at[core], h_ref.at[own, :]),
        (cov.at[core], z_ref.at[:, own]),
    ]
    local = [
        pltpu.make_async_copy(src, dst, lsem.at[i]) for i, (src, dst) in enumerate(own_blocks)
    ]
    for copy in local:
        copy.start()
    sends = [
        (space, k_ref.at[own, :]),
        (data.at[1 - core], h_ref.at[own, :]),
        (cov.at[1 - core], z_ref.at[:, own]),
    ]
    remote = [
        pltpu.make_async_remote_copy(
            src_ref=src,
            dst_ref=dst,
            send_sem=ssem.at[i],
            recv_sem=rsem.at[i],
            device_id=peer,
            device_id_type=MESH,
        )
        for i, (src, dst) in enumerate(sends)
    ]
    pl.semaphore_wait(barrier, 1)
    for copy in remote:
        copy.start()
    day = 2 * lax.axis_index("tm") + core
    days = 2 * lax.axis_size("tm")
    shape = (1, c_ref.shape[1])
    tau = jnp.exp(jnp.broadcast_to(hyper[0:1, 0:1], shape))
    rho = jnp.tanh(jnp.broadcast_to(hyper[0:1, 1:2], shape))
    noise = jnp.exp(jnp.broadcast_to(hyper[0:1, 2:3], shape))
    border = (day == 0) | (day == days - 1)
    scale = tau * jnp.where(border, 1.0, 1.0 + rho * rho)
    c_ref[...] = jnp.concatenate([tau, rho, noise, scale, jnp.zeros((4, shape[1]), F32)], axis=0)
    for copy in local:
        copy.wait()
    for copy in remote:
        copy.wait()
    a_ref[...] = scale * k_ref[...] + noise * h_ref[...]


def growth(bound, steps):
    factors = [2.0 / (2.0 - bound)]
    size = bound / (2.0 - bound)
    for _ in range(steps):
        top = size * size
        factors.append(2.0 / (2.0 - top))
        size = top / (2.0 - top)
    return factors


def warm_inverse(a, old, delta, bound, steps):
    n = a.shape[0]
    diag = diagonal(n)
    c = growth(bound, steps)

    def shifted(factor, m):
        m = factor * m
        return jnp.where(diag, m + (1.0 - factor), m)

    high, low = old if isinstance(old, tuple) else split(old)
    e = shifted(c[0], nn((high, low), delta)).astype(BF16)
    p = (c[0] * c[1]) * (e.astype(F32) + eye(n))
    for step in range(1, steps):
        e = shifted(c[step], bdot(e, e)).astype(BF16)
        p = p + bdot(e, p)
        if step < steps - 1:
            p = c[step + 1] * p
    x = bdot(p, high) + bdot(p, low)
    residual = eye(n) - nn(x, a)
    return x + bdot(residual, x)


def pack(ref, x):
    half = x.shape[0] // 2
    row = lax.broadcasted_iota(jnp.int32, (half, half), 0)
    col = lax.broadcasted_iota(jnp.int32, (half, half), 1)
    first = x[:half, :half]
    ref[pl.ds(0, half), pl.ds(0, half)] = x[half:, :half]
    ref[pl.ds(0, half), pl.ds(half, half)] = jnp.where(row > col, first, x[half:, half:])
    line = jnp.sum(jnp.where(row == col, first, 0.0), axis=0, keepdims=True)
    ref[pl.ds(half, 8), :] = jnp.broadcast_to(jnp.concatenate([line, line], axis=1), (8, 2 * half))


def unpack(ref):
    half = ref.shape[-1] // 2
    row = lax.broadcasted_iota(jnp.int32, (half, half), 0)
    col = lax.broadcasted_iota(jnp.int32, (half, half), 1)
    low = ref[pl.ds(0, half), pl.ds(0, half)]
    fold = ref[pl.ds(0, half), pl.ds(half, half)]
    line = ref[pl.ds(half, 1), pl.ds(0, half)]
    turned = fold.T
    first = jnp.where(row > col, fold, jnp.where(row == col, line, turned))
    last = jnp.where(row > col, turned, fold)
    return jnp.concatenate(
        [jnp.concatenate([first, low.T], axis=1), jnp.concatenate([low, last], axis=1)], axis=0
    )


def total(m):
    return jnp.sum(jnp.sum(m, axis=0, keepdims=True), axis=1, keepdims=True)


def slots(levels):
    names = ["w0", "w1", "w2", "w3", "v0", "v1", "part", "n", "yn", "m", "ym", "x", "y", "g", "sigma", "ea", "ex"]
    for level in range(levels):
        names += [f"{kind}{level}{side}" for kind in "xsl" for side in "ab"]
    return {name: i for i, name in enumerate(names)}


def main_kernel(levels, c_ref, k_ref, h_ref, z_ref, x0_ref, a0_ref, prior_ref, *rest):
    out_ref, grad_ref, fixed_ref = rest[:3]
    wo, wi, vo, vi, to, ti, xo, xi, so, si, lo, li = rest[3:15]
    qo, qi, yo, yi, parts, xfin, xhalf, yfin, ypeer, tiles, sig, ea, ex, s0_ref, ssem, rsem, psend, precv = rest[15:]
    n = 1 << levels
    extent = k_ref.shape[0]
    core = lax.axis_index("blk")
    m = lax.axis_index("tm")
    half = out_ref.shape[1]
    f = z_ref.shape[0]
    number = slots(levels)

    barrier = pltpu.get_barrier_semaphore()

    @pl.loop(1, 2 * n)
    def _(o):
        t = (2 * m + core + o) % (2 * n)
        pl.semaphore_signal(
            barrier, inc=1, device_id={"tm": t // 2, "blk": t % 2}, device_id_type=MESH
        )

    def copy(name, src, dst, chip, side):
        return pltpu.make_async_remote_copy(
            src_ref=src,
            dst_ref=dst,
            send_sem=ssem.at[number[name]],
            recv_sem=rsem.at[number[name]],
            device_id={"tm": (chip + n) % n, "blk": side},
            device_id_type=MESH,
        )

    pending = {0: [], 1: []}

    def send(own, name, src, dst, chip, side, flag=None):
        transfer = copy(name, src, dst, chip, side)
        if flag is None:
            transfer.start()
        else:
            pl.when(flag)(transfer.start)
        pending[own].append((transfer, flag))

    def receive(own, name, dst, flag=None):
        transfer = copy(name, dst, dst, m, 1 - own)
        if flag is None:
            transfer.wait_recv()
            return
        pl.when(flag)(transfer.wait_recv)

        @pl.when(jnp.logical_not(flag))
        def _():
            dst[...] = jnp.zeros_like(dst)

    def drain(own, keep=0):
        done = len(pending[own]) - keep
        for transfer, flag in pending[own][:done]:
            if flag is None:
                transfer.wait_send()
            else:
                pl.when(flag)(transfer.wait_send)
        del pending[own][:done]

    def packet(to, slot):
        return pltpu.make_async_remote_copy(
            src_ref=parts.at[m],
            dst_ref=parts.at[slot],
            send_sem=psend.at[to],
            recv_sem=precv.at[slot],
            device_id={"tm": to, "blk": 0},
            device_id_type=MESH,
        )

    def arrow():
        s0 = c_ref[2:3, :] * nn(z_ref[...], h_ref[...])
        s0_ref[...] = s0
        return s0

    def couple():
        return (c_ref[0:1, :] * c_ref[1:2, :]) * k_ref[...]

    def odd():
        k = couple()
        k_parts = split(k)
        x0 = x0_ref[...]
        p = nn(k_parts, x0)
        pack(wo, nt(p, k_parts))
        pl.semaphore_wait(barrier, 2 * n - 1)
        send(1, "w1", wo, wi.at[1], m + 1, 0, m + 1 < n)
        send(1, "w0", wo, wi.at[0], m, 0)
        s0 = arrow()
        vo[...] = nt(s0, p)
        send(1, "v1", vo, vi.at[1], m + 1, 0, m + 1 < n)
        send(1, "v0", vo, vi.at[0], m, 0)
        send(1, "w2", wo, wi.at[2], m - 1, 0, (m >= 1) & (m < n - 1))
        send(1, "w3", wo, wi.at[3], m + 2, 0, m + 2 < n)
        part = nt(s0, z_ref[...]) - nt(nn(s0, x0), s0)
        to[...] = fold(part)
        send(1, "part", to, ti, m, 0)
        bound, steps = (0.83, 3) if levels < 4 else (0.96, 4)
        drain(1)
        receive(1, "ea", ea)
        receive(1, "ex", ex)
        receive(1, "m", qi.at[0])
        f_even = unpack(qi.at[0])
        before = warm_inverse(ea[...] - f_even, ex[...], f_even, 0.5, 2)
        f_own = nt(nn(k, before), k)
        a = a0_ref[...] - f_own
        x = warm_inverse(a, x0, f_own, bound, steps)
        receive(1, "ym", yi.at[0])
        s_left = nt(nn(yi[0], before), k)
        x_parts = split(x)
        receive(1, "n", qi.at[1], m < n - 1)
        b_own = nt(nn(k_parts, unpack(qi.at[1])), k_parts)
        receive(1, "yn", yi.at[1], m < n - 1)
        s = s0 + (s_left + nt(yi[1], k))
        x = warm_inverse(a - b_own, x_parts, b_own, bound, steps)
        xfin[...] = x
        swap(1)
        y = nn(s, x)
        yfin[...] = y
        send(1, "y", yfin, ypeer, m, 0)
        share(1, x, y, f_own, s_left)
        receive(1, "sigma", sig)
        finish(1, x, y, unfold(sig[...], f))

    def even():
        pl.semaphore_wait(barrier, 2 * n - 1)
        s0 = arrow()
        send(0, "ea", a0_ref, ea, m, 1)
        send(0, "ex", x0_ref, ex, m, 1)
        receive(0, "w1", wi.at[1], m >= 1)
        receive(0, "w0", wi.at[0])
        x0 = x0_ref[...]
        a0 = a0_ref[...]
        f_own = unpack(wi.at[1])
        b_own = unpack(wi.at[0])
        delta = f_own + b_own
        a = a0 - delta
        x = warm_inverse(a, x0, delta, 0.75, 3)
        l = -f_own
        u = jnp.where(m < n - 1, -1.0, 0.0) * b_own
        for level in range(levels + 1):
            d = 1 << level
            if level < levels:
                pack(xo.at[level], x)
                send(0, f"x{level}a", xo.at[level], xi.at[2 * level], m + d, 0, m + d < n)
                send(0, f"x{level}b", xo.at[level], xi.at[2 * level + 1], m - d, 0, m >= d)
            else:
                pack(qo.at[0], f_own)
                send(0, "m", qo.at[0], qi.at[0], m, 1)
                ahead = warm_inverse(a0 - b_own, x0, b_own, 0.5, 2)
                pack(qo.at[1], ahead)
                send(0, "n", qo.at[1], qi.at[1], m - 1, 1, m >= 1)
            if level == 0:
                receive(0, "v1", vi.at[1], m >= 1)
                receive(0, "v0", vi.at[0])
                s_left = vi[1]
                s_right = vi[0]
                s_first = s0 + s_left + s_right
            else:
                back = d // 2
                receive(0, f"s{level - 1}a", si.at[2 * level - 2], m >= back)
                receive(0, f"s{level - 1}b", si.at[2 * level - 1], m + back < n)
                s_left = s_left - nt(si[2 * level - 2], p)
                s_right = s_right - nt(si[2 * level - 1], q)
            s = s0 + s_left + s_right
            if level == levels:
                break
            so[level] = s
            send(0, f"s{level}a", so.at[level], si.at[2 * level], m + d, 0, m + d < n)
            send(0, f"s{level}b", so.at[level], si.at[2 * level + 1], m - d, 0, m >= d)
            if 0 < level < levels:
                if level == 1:
                    receive(0, "w3", wi.at[3], m >= 2)
                    receive(0, "w2", wi.at[2], m < n - 2)
                    l_far = -unpack(wi.at[3])
                    u_far = -unpack(wi.at[2])
                else:
                    lr, ur = li.at[2 * level - 4], li.at[2 * level - 3]
                    receive(0, f"l{level - 1}a", lr, m >= back)
                    receive(0, f"l{level - 1}b", ur, m + back < n)
                    l_far, u_far = lr[...], ur[...]
                l = -nn(p, l_far)
                u = -nn(q, u_far)
            if 0 < level < levels - 1:
                ls, us = lo.at[2 * level - 2], lo.at[2 * level - 1]
                ls[...] = l
                us[...] = u
                send(0, f"l{level}a", ls, li.at[2 * level - 2], m + d, 0, m + d < n)
                send(0, f"l{level}b", us, li.at[2 * level - 1], m - d, 0, m >= d)
            l_parts, u_parts, x_parts = split(l), split(u), split(x)
            drain(0, 6 if 0 < level < levels - 1 else 4)
            receive(0, f"x{level}a", xi.at[2 * level], m >= d)
            receive(0, f"x{level}b", xi.at[2 * level + 1], m + d < n)
            p = nn(l_parts, unpack(xi.at[2 * level]))
            q = nn(u_parts, unpack(xi.at[2 * level + 1]))
            d_left = nt(p, l_parts)
            d_right = nt(q, u_parts)
            f_own = f_own + d_left
            b_own = b_own + d_right
            delta = d_left + d_right
            a = a - delta
            if level < levels - 1:
                x = warm_inverse(a, x_parts, delta, 0.75, 3)
        yo[1] = nn(s0 + s_right, ahead)
        send(0, "yn", yo.at[1], yi.at[1], m - 1, 1, m >= 1)
        yo[0] = s0 + s_left
        send(0, "ym", yo.at[0], yi.at[0], m, 1)
        x = warm_inverse(a, x, delta, 0.5, 3)
        xfin[...] = x
        swap(0)
        y = nn(s, x)
        receive(0, "part", ti)
        own = nt(s0, z_ref[...]) - nt(y, s_first)
        parts[m] = fold(own) + ti[...]

        @pl.loop(1, n)
        def _(o):
            packet((m + o) % n, m).start()

        yfin[...] = y
        send(0, "y", yfin, ypeer, m, 1)
        share(0, x, y, f_own, s_left)

        drain(0, 3)

        @pl.loop(1, n)
        def _(o):
            packet((m + o) % n, m).wait_send()

        @pl.loop(1, n)
        def _(o):
            packet(m, (m + o) % n).wait_recv()

        sigma = spd_inverse(eye(f) * prior_ref[...] + unfold(jnp.sum(parts[...], axis=0), f))
        sig[...] = fold(sigma)
        send(0, "sigma", sig, sig, m, 1)
        finish(0, x, y, sigma)

    def swap(own):
        src = xfin.at[pl.ds((1 - own) * half, half), :]
        send(own, "x", src, xhalf, m, 1 - own)

    def share(own, x, y, f_own, s_left):
        day = 2 * m + own
        k, h = k_ref[...], h_ref[...]
        sides = [nn(y, k), nn(y, h), nn(y, f_own) + s_left, -s0_ref[...]]
        gram = nt(jnp.concatenate(sides, axis=0), y)
        grams = [gram[i * f : (i + 1) * f] for i in range(4)]
        sums = [total(x * k), total(x * h), total(x * f_own), jnp.zeros((1, 1), F32)]
        for i, gram in enumerate(gradients_of(c_ref, *grams, day, 2 * n, extent)):
            tiles[own, i] = fold(gram)
        base = gradients_of(c_ref, *sums, day, 2 * n, extent)
        line = lax.broadcasted_iota(jnp.int32, (8, 4 * f), 0)
        tiles[own, 3] = jnp.where(line == 0, base[0], jnp.where(line == 1, base[1], base[2]))
        send(own, "g", tiles.at[own], tiles.at[own], m, 1 - own)

    def finish(own, x, y, sigma):
        fixed_ref[...] = sigma
        rows = slice(own * half, (own + 1) * half)
        out_ref[own] = x[rows, :] + tn(y[:, rows], nn(sigma, y))
        receive(own, "y", ypeer)
        y_peer = ypeer[...]
        update = tn(y_peer[:, rows], nn(sigma, y_peer))
        receive(own, "x", xhalf)
        out_ref[1 - own] = xhalf[...] + update
        receive(own, "g", tiles.at[1 - own])
        flat = fold(sigma)
        two = lax.broadcasted_iota(jnp.int32, (2, 3), 0)
        col = lax.broadcasted_iota(jnp.int32, (2, 3), 1)
        grads = jnp.zeros((2, 3), F32)
        for side in range(2):
            for i in range(3):
                value = tiles[side, 3, i : i + 1, 0:1] + total(flat * tiles[side, i])
                grads = jnp.where((col == i) & (two == side), value, grads)
        grad_ref[...] = grads
        drain(own)

    pl.when(core == 1)(odd)
    pl.when(core == 0)(even)


def fold(t):
    n = t.shape[0]
    return jnp.concatenate([t[i : i + 8] for i in range(0, n, 8)], axis=1)


def unfold(t, n):
    return jnp.concatenate([t[:, i : i + n] for i in range(0, n * n // 8, n)], axis=0)


def small_inverse(a, b, c, d):
    scale = 1.0 / (a * d - b * c)
    return d * scale, -b * scale, -c * scale, a * scale


def small_product(x, y):
    return (
        x[0] * y[0] + x[1] * y[2],
        x[0] * y[1] + x[1] * y[3],
        x[2] * y[0] + x[3] * y[2],
        x[2] * y[1] + x[3] * y[3],
    )


def spd_inverse(m):
    n = m.shape[0]
    rows = lax.broadcasted_iota(jnp.int32, (n, n), 0)
    cols = lax.broadcasted_iota(jnp.int32, (n, n), 1)
    line = cols[0:1]
    diag = jnp.where(rows == cols, m, 0.0)
    scale = lax.rsqrt(jnp.sum(diag, axis=0, keepdims=True)) * lax.rsqrt(
        jnp.sum(diag, axis=1, keepdims=True)
    )
    m = m * scale
    for k in range(0, n, 4):
        col = [jnp.broadcast_to(m[:, k + i : k + i + 1], (n, n)) for i in range(4)]
        pivot = [[col[j][k + i : k + i + 1, :] for j in range(4)] for i in range(4)]
        row = []
        for i in range(4):
            r = m[k + i : k + i + 1, :]
            for j in range(4):
                r = jnp.where(line == k + j, 1.0 if i == j else 0.0, r)
            row.append(r)
        a, b, c, d = [
            (pivot[i][j], pivot[i][j + 1], pivot[i + 1][j], pivot[i + 1][j + 1])
            for i in (0, 2)
            for j in (0, 2)
        ]
        a_inv = small_inverse(*a)
        ca = small_product(c, a_inv)
        ab = small_product(a_inv, b)
        schur = small_inverse(*[x - y for x, y in zip(d, small_product(ca, b))])
        low0 = row[2] - (ca[0] * row[0] + ca[1] * row[1])
        low1 = row[3] - (ca[2] * row[0] + ca[3] * row[1])
        t2 = schur[0] * low0 + schur[1] * low1
        t3 = schur[2] * low0 + schur[3] * low1
        t0 = a_inv[0] * row[0] + a_inv[1] * row[1] - (ab[0] * t2 + ab[1] * t3)
        t1 = a_inv[2] * row[0] + a_inv[3] * row[1] - (ab[2] * t2 + ab[3] * t3)
        in_rows = (rows >= k) & (rows < k + 4)
        m = jnp.where(in_rows | ((cols >= k) & (cols < k + 4)), 0.0, m)
        for i, t in enumerate((t0, t1, t2, t3)):
            m = m - jnp.where(in_rows, jnp.where(rows == k + i, -1.0, 0.0), col[i]) * t
    return m * scale


def gradients_of(c_ref, k_sum, h_sum, f_sum, u_sum, day, days, extent):
    tau, rho, noise = c_ref[0:1, 0:1], c_ref[1:2, 0:1], c_ref[2:3, 0:1]
    comp = 1.0 - rho * rho
    chain = f_sum / (tau * rho)
    border = (day == 0) | (day == days - 1)
    a_day = jnp.where(border, 1.0, 1.0 + rho * rho)
    b_day = jnp.where(border, 0.0, 2.0 * rho * comp)
    return [
        (tau * a_day * k_sum - 2.0 * tau * rho * chain) / extent,
        (tau * b_day * k_sum - 2.0 * tau * comp * chain) / extent,
        (noise * h_sum + 2.0 * u_sum) / extent,
    ]


def store_kernel(day_ref, grad_ref, fixed_ref, day_out, grad_out, fixed_out, sem):
    pairs = [(day_ref, day_out), (grad_ref, grad_out), (fixed_ref, fixed_out)]
    copies = [pltpu.make_async_copy(src, dst, sem.at[i]) for i, (src, dst) in enumerate(pairs)]
    for copy in copies:
        copy.start()
    for copy in copies:
        copy.wait()


def shaped(*shapes):
    return [jax.ShapeDtypeStruct(s, F32) for s in shapes]


def on_device(hyper_params, space_precision, data_precision, covariates, fixed_precision):
    n = lax.axis_size("tm")
    levels = n.bit_length() - 1
    half, extent = space_precision.shape
    fixed = covariates.shape[1]
    square = (extent, extent)
    side = (fixed, extent)
    packed = (half + 8, extent)
    far = max(2 * (levels - 2), 2)
    ready = pl.pallas_call(
        ready_kernel,
        out_shape=shaped((8, 128))[0],
        in_specs=[],
        out_specs=VMEM,
        compiler_params=pltpu.CompilerParams(vmem_limit_bytes=16 * MIB),
        cost_estimate=pl.CostEstimate(flops=COST, bytes_accessed=8 * extent, transcendentals=0),
    )()
    c, k, h, z, a = pl.pallas_call(
        exchange_kernel,
        out_shape=shaped((8, extent), square, square, side, square),
        in_specs=[VMEM] * 2 + [HBM] * 3,
        out_specs=[VMEM] * 5,
        scratch_shapes=[pltpu.SemaphoreType.DMA((3,))] * 3,
        compiler_params=pltpu.CompilerParams(
            collective_id=0, has_side_effects=True, vmem_limit_bytes=16 * MIB
        ),
    )(ready, hyper_params[None], space_precision, data_precision, covariates)
    x = pl.pallas_call(
        first_kernel,
        out_shape=shaped(square)[0],
        in_specs=[VMEM],
        out_specs=VMEM,
        scratch_shapes=[pltpu.VMEM(square, F32)],
        compiler_params=pltpu.CompilerParams(vmem_limit_bytes=16 * MIB),
    )(a)
    count = len(slots(levels))
    buffers = [
        packed,
        (4,) + packed,
        side,
        (2,) + side,
        (8, 4 * fixed),
        (8, 4 * fixed),
        (levels,) + packed,
        (2 * levels,) + packed,
        (levels,) + side,
        (2 * levels,) + side,
        (far,) + square,
        (far,) + square,
        (2,) + packed,
        (2,) + packed,
        (2,) + side,
        (2,) + side,
        (n, 8, 4 * fixed),
        square,
        (half, extent),
        side,
        side,
        (2, 4, 8, 4 * fixed),
        (8, 4 * fixed),
        square,
        square,
        side,
    ]
    results = pl.pallas_call(
        functools.partial(main_kernel, levels),
        out_shape=shaped((2, half, extent), (2, 3), (fixed, fixed)),
        in_specs=[VMEM] * 7,
        out_specs=[VMEM] * 3,
        scratch_shapes=[pltpu.VMEM(shape, F32) for shape in buffers]
        + [
            pltpu.SemaphoreType.DMA((count,)),
            pltpu.SemaphoreType.DMA((count,)),
            pltpu.SemaphoreType.DMA((n,)),
            pltpu.SemaphoreType.DMA((n,)),
        ],
        compiler_params=pltpu.CompilerParams(
            collective_id=1, has_side_effects=True, vmem_limit_bytes=40 * MIB
        ),
    )(c, k, h, z, x, a, fixed_precision[None])
    days, grads, sigma = pl.pallas_call(
        store_kernel,
        out_shape=shaped((2, half, extent), (2, 3), (fixed, fixed)),
        in_specs=[VMEM] * 3,
        out_specs=[HBM] * 3,
        scratch_shapes=[pltpu.SemaphoreType.DMA((3,))],
        compiler_params=pltpu.CompilerParams(vmem_limit_bytes=4 * MIB),
    )(*results)
    return days, grads.T, sigma


def solution(mesh):
    in_specs = (
        P("grp"),
        P("blk", None),
        P(("grp", "tm"), "blk", None),
        P(("grp", "tm"), None, "blk"),
        P("grp"),
    )
    out_specs = (P(("grp", "tm"), "blk", None), P(None, ("grp", "tm")), P("grp", None))
    return jax.shard_map(
        on_device, mesh=mesh, in_specs=in_specs, out_specs=out_specs, check_vma=False
    )
```

```python
import functools

import jax
import jax.numpy as jnp
from jax import lax
from jax.experimental import pallas as pl
from jax.experimental.pallas import tpu as pltpu
from jax.sharding import PartitionSpec as P

HIGHEST = lax.Precision.HIGHEST
F32 = jnp.float32
BF16 = jnp.bfloat16
VMEM = pl.BlockSpec(memory_space=pltpu.VMEM)
HBM = pl.BlockSpec(memory_space=pltpu.HBM)
CLOSE = 1e-6
STEPS = 40
MESH = pl.DeviceIdType.MESH
MIB = 1024 * 1024
COST = 2**32


def split(a):
    high = a.astype(BF16)
    return high, (a - high.astype(F32)).astype(BF16)


def bdot(a, b):
    return jnp.dot(a.astype(BF16), b.astype(BF16), preferred_element_type=F32)


def contract(dims):
    def dot(a, b):
        def one(p, q):
            return lax.dot_general(p, q, (dims, ((), ())), preferred_element_type=F32)

        ah, al = a if isinstance(a, tuple) else split(a)
        bh, bl = b if isinstance(b, tuple) else split(b)
        return one(ah, bh) + (one(ah, bl) + one(al, bh))

    return dot


nn = contract(((1,), (0,)))
nt = contract(((1,), (1,)))
tn = contract(((0,), (0,)))


def full_dot(a, b):
    return jnp.dot(a, b, precision=HIGHEST, preferred_element_type=F32)


def diagonal(n):
    return lax.broadcasted_iota(jnp.int32, (n, n), 0) == lax.broadcasted_iota(jnp.int32, (n, n), 1)


def eye(n):
    return diagonal(n).astype(F32)


def squares(r):
    return jnp.sum(r * r)


def safe_start(a):
    unit = eye(a.shape[0])
    diag_row = jnp.sum(a * unit, axis=0, keepdims=True)
    diag_col = jnp.sum(a * unit, axis=1, keepdims=True)
    scaled = jnp.abs(a) * lax.rsqrt(diag_row) * lax.rsqrt(diag_col)
    bound = jnp.max(jnp.sum(scaled, axis=0, keepdims=True))
    return unit / (diag_row * bound)


def series(x_ref, r_ref):
    def more(state):
        count, size = state
        return (count < 12) & (size > 1e-4)

    def step(state):
        count, _ = state
        r = r_ref[...].astype(BF16)
        x_ref[...] += jnp.dot(r, x_ref[...].astype(BF16), preferred_element_type=F32)
        r_new = jnp.dot(r, r, preferred_element_type=F32)
        r_ref[...] = r_new
        return count + 1, squares(r_new)

    lax.while_loop(more, step, (0, squares(r_ref[...])))


def polish(a, x_ref):
    unit = eye(a.shape[0])

    def more(state):
        count, size, before = state
        return (count < STEPS) & (size > CLOSE) & ((size < before) | (size > 0.5))

    def step(state):
        count, size, _ = state
        r = unit - full_dot(a, x_ref[...])
        new = squares(r)
        restart = (count == 0) & ~(new < 0.8)

        @pl.when(restart)
        def _():
            x_ref[...] = safe_start(a)

        @pl.when(jnp.logical_not(restart))
        def _():
            x_ref[...] += nn(x_ref[...], r)

        return count + 1, jnp.where(restart, 1e30, new), jnp.where(restart, 2e30, size)

    lax.while_loop(more, step, (0, jnp.float32(1e30), jnp.float32(2e30)))


def first_kernel(a_ref, x_ref, r_ref):
    a = a_ref[...]
    n = a.shape[0]
    unit = eye(n)
    diag_row = jnp.sum(a * unit, axis=0, keepdims=True)
    diag_col = jnp.sum(a * unit, axis=1, keepdims=True)
    inv_col = 1.0 / diag_col
    turned = a * inv_col
    weight = n / total(turned * a * (1.0 / diag_row))
    e = unit - weight * turned
    p = unit + e
    for _ in range(3):
        e = e.astype(BF16)
        e = bdot(e, e)
        p = p + bdot(e, p)
    x = p * (weight / diag_row)
    x = x + bdot(unit - nn(x, a), x)
    residual = unit - nn(x, a)
    x_ref[...] = x + bdot(residual, x)

    @pl.when(jnp.logical_not(squares(residual) < 1e-5))
    def _():
        start = safe_start(a)
        x_ref[...] = start
        r_ref[...] = unit - jnp.sum(start, axis=1, keepdims=True) * a
        series(x_ref, r_ref)
        polish(a, x_ref)


def ready_kernel(ready_ref):
    ready_ref[...] = jnp.zeros_like(ready_ref)


def exchange_kernel(ready_ref, hyper, space, data, cov, c_ref, k_ref, h_ref, z_ref, a_ref, *sems):
    ssem, rsem, lsem = sems
    core = lax.axis_index("blk")
    peer = {"blk": 1 - core}
    half = space.shape[0]
    barrier = pltpu.get_barrier_semaphore()
    pl.semaphore_signal(barrier, inc=1, device_id=peer, device_id_type=MESH)
    own = pl.ds(pl.multiple_of(core * half, half), half)
    own_blocks = [
        (space, k_ref.at[own, :]),
        (data.at[core], h_ref.at[own, :]),
        (cov.at[core], z_ref.at[:, own]),
    ]
    local = [
        pltpu.make_async_copy(src, dst, lsem.at[i]) for i, (src, dst) in enumerate(own_blocks)
    ]
    for copy in local:
        copy.start()
    sends = [
        (space, k_ref.at[own, :]),
        (data.at[1 - core], h_ref.at[own, :]),
        (cov.at[1 - core], z_ref.at[:, own]),
    ]
    remote = [
        pltpu.make_async_remote_copy(
            src_ref=src,
            dst_ref=dst,
            send_sem=ssem.at[i],
            recv_sem=rsem.at[i],
            device_id=peer,
            device_id_type=MESH,
        )
        for i, (src, dst) in enumerate(sends)
    ]
    pl.semaphore_wait(barrier, 1)
    for copy in remote:
        copy.start()
    day = 2 * lax.axis_index("tm") + core
    days = 2 * lax.axis_size("tm")
    shape = (1, c_ref.shape[1])
    tau = jnp.exp(jnp.broadcast_to(hyper[0:1, 0:1], shape))
    rho = jnp.tanh(jnp.broadcast_to(hyper[0:1, 1:2], shape))
    noise = jnp.exp(jnp.broadcast_to(hyper[0:1, 2:3], shape))
    border = (day == 0) | (day == days - 1)
    scale = tau * jnp.where(border, 1.0, 1.0 + rho * rho)
    c_ref[...] = jnp.concatenate([tau, rho, noise, scale, jnp.zeros((4, shape[1]), F32)], axis=0)
    for copy in local:
        copy.wait()
    for copy in remote:
        copy.wait()
    a_ref[...] = scale * k_ref[...] + noise * h_ref[...]


def growth(bound, steps):
    factors = [2.0 / (2.0 - bound)]
    size = bound / (2.0 - bound)
    for _ in range(steps):
        top = size * size
        factors.append(2.0 / (2.0 - top))
        size = top / (2.0 - top)
    return factors


def warm_inverse(a, old, delta, bound, steps):
    n = a.shape[0]
    diag = diagonal(n)
    c = growth(bound, steps)

    def shifted(factor, m):
        m = factor * m
        return jnp.where(diag, m + (1.0 - factor), m)

    high, low = old if isinstance(old, tuple) else split(old)
    e = shifted(c[0], nn((high, low), delta)).astype(BF16)
    p = (c[0] * c[1]) * (e.astype(F32) + eye(n))
    for step in range(1, steps):
        e = shifted(c[step], bdot(e, e)).astype(BF16)
        p = p + bdot(e, p)
        if step < steps - 1:
            p = c[step + 1] * p
    x = bdot(p, high) + bdot(p, low)
    residual = eye(n) - nn(x, a)
    return x + bdot(residual, x)


def pack(ref, x):
    half = x.shape[0] // 2
    row = lax.broadcasted_iota(jnp.int32, (half, half), 0)
    col = lax.broadcasted_iota(jnp.int32, (half, half), 1)
    first = x[:half, :half]
    ref[pl.ds(0, half), pl.ds(0, half)] = x[half:, :half]
    ref[pl.ds(0, half), pl.ds(half, half)] = jnp.where(row > col, first, x[half:, half:])
    line = jnp.sum(jnp.where(row == col, first, 0.0), axis=0, keepdims=True)
    ref[pl.ds(half, 8), :] = jnp.broadcast_to(jnp.concatenate([line, line], axis=1), (8, 2 * half))


def unpack(ref):
    half = ref.shape[-1] // 2
    row = lax.broadcasted_iota(jnp.int32, (half, half), 0)
    col = lax.broadcasted_iota(jnp.int32, (half, half), 1)
    low = ref[pl.ds(0, half), pl.ds(0, half)]
    fold = ref[pl.ds(0, half), pl.ds(half, half)]
    line = ref[pl.ds(half, 1), pl.ds(0, half)]
    turned = fold.T
    first = jnp.where(row > col, fold, jnp.where(row == col, line, turned))
    last = jnp.where(row > col, turned, fold)
    return jnp.concatenate(
        [jnp.concatenate([first, low.T], axis=1), jnp.concatenate([low, last], axis=1)], axis=0
    )


def total(m):
    return jnp.sum(jnp.sum(m, axis=0, keepdims=True), axis=1, keepdims=True)


def slots(levels):
    names = ["w0", "w1", "w2", "w3", "v0", "v1", "part", "n", "yn", "m", "ym", "x", "y", "g", "sigma", "ea", "ex"]
    for level in range(levels):
        names += [f"{kind}{level}{side}" for kind in "xsl" for side in "ab"]
    return {name: i for i, name in enumerate(names)}


def main_kernel(levels, c_ref, k_ref, h_ref, z_ref, x0_ref, a0_ref, prior_ref, *rest):
    out_ref, grad_ref, fixed_ref = rest[:3]
    wo, wi, vo, vi, to, ti, xo, xi, so, si, lo, li = rest[3:15]
    qo, qi, yo, yi, parts, xfin, xhalf, yfin, ypeer, tiles, sig, ea, ex, s0_ref, ssem, rsem, psend, precv = rest[15:]
    n = 1 << levels
    extent = k_ref.shape[0]
    core = lax.axis_index("blk")
    m = lax.axis_index("tm")
    half = out_ref.shape[1]
    f = z_ref.shape[0]
    number = slots(levels)

    barrier = pltpu.get_barrier_semaphore()

    def greet(chip, side, flag=None):
        def signal():
            target = {"tm": (chip + n) % n, "blk": side}
            pl.semaphore_signal(barrier, inc=1, device_id=target, device_id_type=MESH)

        if flag is None:
            signal()
        else:
            pl.when(flag)(signal)

    def greeted(sure, *flags):
        pl.semaphore_wait(barrier, sure + sum(jnp.where(flag, 1, 0) for flag in flags))

    def copy(name, src, dst, chip, side):
        return pltpu.make_async_remote_copy(
            src_ref=src,
            dst_ref=dst,
            send_sem=ssem.at[number[name]],
            recv_sem=rsem.at[number[name]],
            device_id={"tm": (chip + n) % n, "blk": side},
            device_id_type=MESH,
        )

    pending = {0: [], 1: []}

    def send(own, name, src, dst, chip, side, flag=None):
        transfer = copy(name, src, dst, chip, side)
        if flag is None:
            transfer.start()
        else:
            pl.when(flag)(transfer.start)
        pending[own].append((transfer, flag))

    def receive(own, name, dst, flag=None):
        transfer = copy(name, dst, dst, m, 1 - own)
        if flag is None:
            transfer.wait_recv()
            return
        pl.when(flag)(transfer.wait_recv)

        @pl.when(jnp.logical_not(flag))
        def _():
            dst[...] = jnp.zeros_like(dst)

    def drain(own, keep=0):
        done = len(pending[own]) - keep
        for transfer, flag in pending[own][:done]:
            if flag is None:
                transfer.wait_send()
            else:
                pl.when(flag)(transfer.wait_send)
        del pending[own][:done]

    def packet(to, slot):
        return pltpu.make_async_remote_copy(
            src_ref=parts.at[m],
            dst_ref=parts.at[slot],
            send_sem=psend.at[to],
            recv_sem=precv.at[slot],
            device_id={"tm": to, "blk": 0},
            device_id_type=MESH,
        )

    def arrow():
        s0 = c_ref[2:3, :] * nn(z_ref[...], h_ref[...])
        s0_ref[...] = s0
        return s0

    def couple():
        return (c_ref[0:1, :] * c_ref[1:2, :]) * k_ref[...]

    def odd():
        greet(m, 0)
        greet(m + 1, 0, m + 1 < n)
        k = couple()
        k_parts = split(k)
        x0 = x0_ref[...]
        p = nn(k_parts, x0)
        pack(wo, nt(p, k_parts))
        greeted(1, m + 1 < n, (m >= 1) & (m < n - 1), m + 2 < n)
        send(1, "w1", wo, wi.at[1], m + 1, 0, m + 1 < n)
        send(1, "w0", wo, wi.at[0], m, 0)
        s0 = arrow()
        vo[...] = nt(s0, p)
        send(1, "v1", vo, vi.at[1], m + 1, 0, m + 1 < n)
        send(1, "v0", vo, vi.at[0], m, 0)
        send(1, "w2", wo, wi.at[2], m - 1, 0, (m >= 1) & (m < n - 1))
        send(1, "w3", wo, wi.at[3], m + 2, 0, m + 2 < n)
        part = nt(s0, z_ref[...]) - nt(nn(s0, x0), s0)
        to[...] = fold(part)
        send(1, "part", to, ti, m, 0)
        bound, steps = (0.83, 3) if levels < 4 else (0.96, 4)
        drain(1)
        receive(1, "ea", ea)
        receive(1, "ex", ex)
        receive(1, "m", qi.at[0])
        f_even = unpack(qi.at[0])
        before = warm_inverse(ea[...] - f_even, ex[...], f_even, 0.5, 2)
        f_own = nt(nn(k, before), k)
        a = a0_ref[...] - f_own
        x = warm_inverse(a, x0, f_own, bound, steps)
        receive(1, "ym", yi.at[0])
        s_left = nt(nn(yi[0], before), k)
        x_parts = split(x)
        receive(1, "n", qi.at[1], m < n - 1)
        b_own = nt(nn(k_parts, unpack(qi.at[1])), k_parts)
        receive(1, "yn", yi.at[1], m < n - 1)
        s = s0 + (s_left + nt(yi[1], k))
        x = warm_inverse(a - b_own, x_parts, b_own, bound, steps)
        xfin[...] = x
        swap(1)
        y = nn(s, x)
        yfin[...] = y
        send(1, "y", yfin, ypeer, m, 0)
        share(1, x, y, f_own, s_left)
        receive(1, "sigma", sig)
        finish(1, x, y, unfold(sig[...], f))

    def even():
        greet(m, 1)
        greet(m - 1, 1, m >= 1)
        greet(m + 1, 1, m < n - 2)
        greet(m - 2, 1, m >= 2)

        @pl.loop(1, n)
        def _(o):
            greet(m + o, 0)

        greeted(n, m >= 1)
        s0 = arrow()
        send(0, "ea", a0_ref, ea, m, 1)
        send(0, "ex", x0_ref, ex, m, 1)
        receive(0, "w1", wi.at[1], m >= 1)
        receive(0, "w0", wi.at[0])
        x0 = x0_ref[...]
        a0 = a0_ref[...]
        f_own = unpack(wi.at[1])
        b_own = unpack(wi.at[0])
        delta = f_own + b_own
        a = a0 - delta
        x = warm_inverse(a, x0, delta, 0.75, 3)
        l = -f_own
        u = jnp.where(m < n - 1, -1.0, 0.0) * b_own
        for level in range(levels + 1):
            d = 1 << level
            if level < levels:
                pack(xo.at[level], x)
                send(0, f"x{level}a", xo.at[level], xi.at[2 * level], m + d, 0, m + d < n)
                send(0, f"x{level}b", xo.at[level], xi.at[2 * level + 1], m - d, 0, m >= d)
            else:
                pack(qo.at[0], f_own)
                send(0, "m", qo.at[0], qi.at[0], m, 1)
                ahead = warm_inverse(a0 - b_own, x0, b_own, 0.5, 2)
                pack(qo.at[1], ahead)
                send(0, "n", qo.at[1], qi.at[1], m - 1, 1, m >= 1)
            if level == 0:
                receive(0, "v1", vi.at[1], m >= 1)
                receive(0, "v0", vi.at[0])
                s_left = vi[1]
                s_right = vi[0]
                s_first = s0 + s_left + s_right
            else:
                back = d // 2
                receive(0, f"s{level - 1}a", si.at[2 * level - 2], m >= back)
                receive(0, f"s{level - 1}b", si.at[2 * level - 1], m + back < n)
                s_left = s_left - nt(si[2 * level - 2], p)
                s_right = s_right - nt(si[2 * level - 1], q)
            s = s0 + s_left + s_right
            if level == levels:
                break
            so[level] = s
            send(0, f"s{level}a", so.at[level], si.at[2 * level], m + d, 0, m + d < n)
            send(0, f"s{level}b", so.at[level], si.at[2 * level + 1], m - d, 0, m >= d)
            if 0 < level < levels:
                if level == 1:
                    receive(0, "w3", wi.at[3], m >= 2)
                    receive(0, "w2", wi.at[2], m < n - 2)
                    l_far = -unpack(wi.at[3])
                    u_far = -unpack(wi.at[2])
                else:
                    lr, ur = li.at[2 * level - 4], li.at[2 * level - 3]
                    receive(0, f"l{level - 1}a", lr, m >= back)
                    receive(0, f"l{level - 1}b", ur, m + back < n)
                    l_far, u_far = lr[...], ur[...]
                l = -nn(p, l_far)
                u = -nn(q, u_far)
            if 0 < level < levels - 1:
                ls, us = lo.at[2 * level - 2], lo.at[2 * level - 1]
                ls[...] = l
                us[...] = u
                send(0, f"l{level}a", ls, li.at[2 * level - 2], m + d, 0, m + d < n)
                send(0, f"l{level}b", us, li.at[2 * level - 1], m - d, 0, m >= d)
            l_parts, u_parts, x_parts = split(l), split(u), split(x)
            drain(0, 6 if 0 < level < levels - 1 else 4)
            receive(0, f"x{level}a", xi.at[2 * level], m >= d)
            receive(0, f"x{level}b", xi.at[2 * level + 1], m + d < n)
            p = nn(l_parts, unpack(xi.at[2 * level]))
            q = nn(u_parts, unpack(xi.at[2 * level + 1]))
            d_left = nt(p, l_parts)
            d_right = nt(q, u_parts)
            f_own = f_own + d_left
            b_own = b_own + d_right
            delta = d_left + d_right
            a = a - delta
            if level < levels - 1:
                x = warm_inverse(a, x_parts, delta, 0.75, 3)
        yo[1] = nn(s0 + s_right, ahead)
        send(0, "yn", yo.at[1], yi.at[1], m - 1, 1, m >= 1)
        yo[0] = s0 + s_left
        send(0, "ym", yo.at[0], yi.at[0], m, 1)
        x = warm_inverse(a, x, delta, 0.5, 3)
        xfin[...] = x
        swap(0)
        y = nn(s, x)
        receive(0, "part", ti)
        own = nt(s0, z_ref[...]) - nt(y, s_first)
        parts[m] = fold(own) + ti[...]

        @pl.loop(1, n)
        def _(o):
            packet((m + o) % n, m).start()

        yfin[...] = y
        send(0, "y", yfin, ypeer, m, 1)
        share(0, x, y, f_own, s_left)

        drain(0, 3)

        @pl.loop(1, n)
        def _(o):
            packet((m + o) % n, m).wait_send()

        @pl.loop(1, n)
        def _(o):
            packet(m, (m + o) % n).wait_recv()

        sigma = spd_inverse(eye(f) * prior_ref[...] + unfold(jnp.sum(parts[...], axis=0), f))
        sig[...] = fold(sigma)
        send(0, "sigma", sig, sig, m, 1)
        finish(0, x, y, sigma)

    def swap(own):
        src = xfin.at[pl.ds((1 - own) * half, half), :]
        send(own, "x", src, xhalf, m, 1 - own)

    def share(own, x, y, f_own, s_left):
        day = 2 * m + own
        k, h = k_ref[...], h_ref[...]
        sides = [nn(y, k), nn(y, h), nn(y, f_own) + s_left, -s0_ref[...]]
        gram = nt(jnp.concatenate(sides, axis=0), y)
        grams = [gram[i * f : (i + 1) * f] for i in range(4)]
        sums = [total(x * k), total(x * h), total(x * f_own), jnp.zeros((1, 1), F32)]
        for i, gram in enumerate(gradients_of(c_ref, *grams, day, 2 * n, extent)):
            tiles[own, i] = fold(gram)
        base = gradients_of(c_ref, *sums, day, 2 * n, extent)
        line = lax.broadcasted_iota(jnp.int32, (8, 4 * f), 0)
        tiles[own, 3] = jnp.where(line == 0, base[0], jnp.where(line == 1, base[1], base[2]))
        send(own, "g", tiles.at[own], tiles.at[own], m, 1 - own)

    def finish(own, x, y, sigma):
        fixed_ref[...] = sigma
        rows = slice(own * half, (own + 1) * half)
        out_ref[own] = x[rows, :] + tn(y[:, rows], nn(sigma, y))
        receive(own, "y", ypeer)
        y_peer = ypeer[...]
        update = tn(y_peer[:, rows], nn(sigma, y_peer))
        receive(own, "x", xhalf)
        out_ref[1 - own] = xhalf[...] + update
        receive(own, "g", tiles.at[1 - own])
        flat = fold(sigma)
        two = lax.broadcasted_iota(jnp.int32, (2, 3), 0)
        col = lax.broadcasted_iota(jnp.int32, (2, 3), 1)
        grads = jnp.zeros((2, 3), F32)
        for side in range(2):
            for i in range(3):
                value = tiles[side, 3, i : i + 1, 0:1] + total(flat * tiles[side, i])
                grads = jnp.where((col == i) & (two == side), value, grads)
        grad_ref[...] = grads
        drain(own)

    pl.when(core == 1)(odd)
    pl.when(core == 0)(even)


def fold(t):
    n = t.shape[0]
    return jnp.concatenate([t[i : i + 8] for i in range(0, n, 8)], axis=1)


def unfold(t, n):
    return jnp.concatenate([t[:, i : i + n] for i in range(0, n * n // 8, n)], axis=0)


def small_inverse(a, b, c, d):
    scale = 1.0 / (a * d - b * c)
    return d * scale, -b * scale, -c * scale, a * scale


def small_product(x, y):
    return (
        x[0] * y[0] + x[1] * y[2],
        x[0] * y[1] + x[1] * y[3],
        x[2] * y[0] + x[3] * y[2],
        x[2] * y[1] + x[3] * y[3],
    )


def spd_inverse(m):
    n = m.shape[0]
    rows = lax.broadcasted_iota(jnp.int32, (n, n), 0)
    cols = lax.broadcasted_iota(jnp.int32, (n, n), 1)
    line = cols[0:1]
    diag = jnp.where(rows == cols, m, 0.0)
    scale = lax.rsqrt(jnp.sum(diag, axis=0, keepdims=True)) * lax.rsqrt(
        jnp.sum(diag, axis=1, keepdims=True)
    )
    m = m * scale
    for k in range(0, n, 4):
        col = [jnp.broadcast_to(m[:, k + i : k + i + 1], (n, n)) for i in range(4)]
        pivot = [[col[j][k + i : k + i + 1, :] for j in range(4)] for i in range(4)]
        row = []
        for i in range(4):
            r = m[k + i : k + i + 1, :]
            for j in range(4):
                r = jnp.where(line == k + j, 1.0 if i == j else 0.0, r)
            row.append(r)
        a, b, c, d = [
            (pivot[i][j], pivot[i][j + 1], pivot[i + 1][j], pivot[i + 1][j + 1])
            for i in (0, 2)
            for j in (0, 2)
        ]
        a_inv = small_inverse(*a)
        ca = small_product(c, a_inv)
        ab = small_product(a_inv, b)
        schur = small_inverse(*[x - y for x, y in zip(d, small_product(ca, b))])
        low0 = row[2] - (ca[0] * row[0] + ca[1] * row[1])
        low1 = row[3] - (ca[2] * row[0] + ca[3] * row[1])
        t2 = schur[0] * low0 + schur[1] * low1
        t3 = schur[2] * low0 + schur[3] * low1
        t0 = a_inv[0] * row[0] + a_inv[1] * row[1] - (ab[0] * t2 + ab[1] * t3)
        t1 = a_inv[2] * row[0] + a_inv[3] * row[1] - (ab[2] * t2 + ab[3] * t3)
        in_rows = (rows >= k) & (rows < k + 4)
        m = jnp.where(in_rows | ((cols >= k) & (cols < k + 4)), 0.0, m)
        for i, t in enumerate((t0, t1, t2, t3)):
            m = m - jnp.where(in_rows, jnp.where(rows == k + i, -1.0, 0.0), col[i]) * t
    return m * scale


def gradients_of(c_ref, k_sum, h_sum, f_sum, u_sum, day, days, extent):
    tau, rho, noise = c_ref[0:1, 0:1], c_ref[1:2, 0:1], c_ref[2:3, 0:1]
    comp = 1.0 - rho * rho
    chain = f_sum / (tau * rho)
    border = (day == 0) | (day == days - 1)
    a_day = jnp.where(border, 1.0, 1.0 + rho * rho)
    b_day = jnp.where(border, 0.0, 2.0 * rho * comp)
    return [
        (tau * a_day * k_sum - 2.0 * tau * rho * chain) / extent,
        (tau * b_day * k_sum - 2.0 * tau * comp * chain) / extent,
        (noise * h_sum + 2.0 * u_sum) / extent,
    ]


def store_kernel(day_ref, grad_ref, fixed_ref, day_out, grad_out, fixed_out, sem):
    pairs = [(day_ref, day_out), (grad_ref, grad_out), (fixed_ref, fixed_out)]
    copies = [pltpu.make_async_copy(src, dst, sem.at[i]) for i, (src, dst) in enumerate(pairs)]
    for copy in copies:
        copy.start()
    for copy in copies:
        copy.wait()


def shaped(*shapes):
    return [jax.ShapeDtypeStruct(s, F32) for s in shapes]


def on_device(hyper_params, space_precision, data_precision, covariates, fixed_precision):
    n = lax.axis_size("tm")
    levels = n.bit_length() - 1
    half, extent = space_precision.shape
    fixed = covariates.shape[1]
    square = (extent, extent)
    side = (fixed, extent)
    packed = (half + 8, extent)
    far = max(2 * (levels - 2), 2)
    ready = pl.pallas_call(
        ready_kernel,
        out_shape=shaped((8, 128))[0],
        in_specs=[],
        out_specs=VMEM,
        compiler_params=pltpu.CompilerParams(vmem_limit_bytes=16 * MIB),
        cost_estimate=pl.CostEstimate(flops=COST, bytes_accessed=8 * extent, transcendentals=0),
    )()
    c, k, h, z, a = pl.pallas_call(
        exchange_kernel,
        out_shape=shaped((8, extent), square, square, side, square),
        in_specs=[VMEM] * 2 + [HBM] * 3,
        out_specs=[VMEM] * 5,
        scratch_shapes=[pltpu.SemaphoreType.DMA((3,))] * 3,
        compiler_params=pltpu.CompilerParams(
            collective_id=0, has_side_effects=True, vmem_limit_bytes=16 * MIB
        ),
    )(ready, hyper_params[None], space_precision, data_precision, covariates)
    x = pl.pallas_call(
        first_kernel,
        out_shape=shaped(square)[0],
        in_specs=[VMEM],
        out_specs=VMEM,
        scratch_shapes=[pltpu.VMEM(square, F32)],
        compiler_params=pltpu.CompilerParams(vmem_limit_bytes=16 * MIB),
    )(a)
    count = len(slots(levels))
    buffers = [
        packed,
        (4,) + packed,
        side,
        (2,) + side,
        (8, 4 * fixed),
        (8, 4 * fixed),
        (levels,) + packed,
        (2 * levels,) + packed,
        (levels,) + side,
        (2 * levels,) + side,
        (far,) + square,
        (far,) + square,
        (2,) + packed,
        (2,) + packed,
        (2,) + side,
        (2,) + side,
        (n, 8, 4 * fixed),
        square,
        (half, extent),
        side,
        side,
        (2, 4, 8, 4 * fixed),
        (8, 4 * fixed),
        square,
        square,
        side,
    ]
    results = pl.pallas_call(
        functools.partial(main_kernel, levels),
        out_shape=shaped((2, half, extent), (2, 3), (fixed, fixed)),
        in_specs=[VMEM] * 7,
        out_specs=[VMEM] * 3,
        scratch_shapes=[pltpu.VMEM(shape, F32) for shape in buffers]
        + [
            pltpu.SemaphoreType.DMA((count,)),
            pltpu.SemaphoreType.DMA((count,)),
            pltpu.SemaphoreType.DMA((n,)),
            pltpu.SemaphoreType.DMA((n,)),
        ],
        compiler_params=pltpu.CompilerParams(
            collective_id=1, has_side_effects=True, vmem_limit_bytes=40 * MIB
        ),
    )(c, k, h, z, x, a, fixed_precision[None])
    days, grads, sigma = pl.pallas_call(
        store_kernel,
        out_shape=shaped((2, half, extent), (2, 3), (fixed, fixed)),
        in_specs=[VMEM] * 3,
        out_specs=[HBM] * 3,
        scratch_shapes=[pltpu.SemaphoreType.DMA((3,))],
        compiler_params=pltpu.CompilerParams(vmem_limit_bytes=4 * MIB),
    )(*results)
    return days, grads.T, sigma


def solution(mesh):
    in_specs = (
        P("grp"),
        P("blk", None),
        P(("grp", "tm"), "blk", None),
        P(("grp", "tm"), None, "blk"),
        P("grp"),
    )
    out_specs = (P(("grp", "tm"), "blk", None), P(None, ("grp", "tm")), P("grp", None))
    return jax.shard_map(
        on_device, mesh=mesh, in_specs=in_specs, out_specs=out_specs, check_vma=False
    )
```
